256 devices in a mesh: dp: 16 (over x, y), tensor: 16 (over z, core).
Axes of the slice: x: 4, y: 4, z: 8, core: 2. Of those that a mesh axis runs over, the one named last changes fastest.
Arguments:
- tokens: bfloat16 [1024, 8192], P('tensor', 'dp'), may hold values from -6 to 6
- grad_output: bfloat16 [1024, 8192], P('tensor', 'dp'), may hold values from -6 to 6
- gate_weight: bfloat16 [8192, 14336], P('dp', 'tensor'), may hold values from -0.09375 to 0.09375
- up_weight: bfloat16 [8192, 14336], P('dp', 'tensor'), may hold values from -0.09375 to 0.09375
- down_weight: bfloat16 [14336, 8192], P('tensor', 'dp'), may hold values from -0.0625 to 0.0625
- gate_mask: int32 [64, 112], P('dp', 'tensor'), may hold values 0 or 1
- up_mask: int32 [64, 112], P('dp', 'tensor'), may hold values 0 or 1
- down_mask: int32 [112, 64], P('tensor', 'dp'), may hold values 0 or 1
Outputs:
- output: bfloat16 [1024, 8192], P('tensor', 'dp')
- grad_tokens: bfloat16 [1024, 8192], P('tensor', 'dp')
- grad_gate: bfloat16 [8192, 14336], P('dp', 'tensor')
- grad_up: bfloat16 [8192, 14336], P('dp', 'tensor')
- grad_down: bfloat16 [14336, 8192], P('tensor', 'dp')
The draws below stay inside these ranges and needn't reach their ends.
All inputs are finite; a program needn't handle non-finite values. No bound on the sum of `gate_mask` or of `up_mask` or of `down_mask` on one device may be relied on, other than what follows from the above.
Results may differ from the reference program's by a relative error of at most 0.005.
Values may be sent and summed in bfloat16 or wider, within the bound.
A program may use at most 128 MiB of HBM per device.

```python
import jax
import jax.numpy as jnp
from jax import lax

D = 8192
FF = 14336
BLOCK = 128
TOKENS = 1024


def with_ends(values, key, low, largest):
    extent = values.shape
    index_at = [jax.random.randint(jax.random.fold_in(key, axis), (), 0, extent[axis]) for axis in range(len(extent))]
    values = values.at[tuple(index_at)].set(low)
    longest = extent.index(max(extent))
    index_at[longest] = (index_at[longest] + 1) % extent[longest]
    return values.at[tuple(index_at)].set(largest)


def levels(rng, shape, pieces, low, top_value):
    def one(axis_at, parts):
        draws = jax.random.uniform(jax.random.fold_in(jax.random.fold_in(rng, 6), axis_at), (parts,), jnp.float32, low / len(pieces), top_value / len(pieces))
        return jnp.repeat(jnp.exp(draws), shape[axis_at] // parts).reshape((-1,) + (1,) * (len(shape) - axis_at - 1))

    loudness = one(*pieces[0])
    for cut in pieces[1:]:
        loudness = loudness * one(*cut)
    return loudness


def scatter_about(key, dims, deviation, reach, cuts=(), dtype=jnp.bfloat16):
    entries = jax.random.normal(key, dims, jnp.float32) * deviation
    if len(cuts) > 0:
        entries = levels(key, dims, cuts, -0.22, 0.18) * entries
    return jnp.clip(entries, min=-reach, max=reach).astype(dtype)


def setup_inputs(seed: int = 0) -> dict:
    arg_keys = jax.random.split(jax.random.key(seed), 9)
    tokens = scatter_about(arg_keys[0], (TOKENS, D), 1.0, 6.0, ((0, 16), (1, 16)))
    grad_output = scatter_about(arg_keys[1], (TOKENS, D), 1.0, 6.0, ((0, 16), (1, 16)))
    gate_weight = scatter_about(arg_keys[2], (D, FF), (D // 2) ** -0.5, 0.09375, ((0, 16), (1, 16)))
    up_weight = scatter_about(arg_keys[3], (D, FF), (D // 2) ** -0.5, 0.09375, ((0, 16), (1, 16)))
    down_weight = scatter_about(arg_keys[4], (FF, D), (FF // 2) ** -0.5, 0.0625, ((0, 16), (1, 16)))
    gate_mask = with_ends((jax.random.randint(arg_keys[5], (D // BLOCK, FF // BLOCK), 0, 2) < 1).astype(jnp.int32), jax.random.fold_in(arg_keys[5], 1), 0, 1)
    up_mask = with_ends((jax.random.randint(arg_keys[6], (D // BLOCK, FF // BLOCK), 0, 2) < 1).astype(jnp.int32), jax.random.fold_in(arg_keys[6], 1), 0, 1)
    down_mask = with_ends((jax.random.randint(arg_keys[7], (FF // BLOCK, D // BLOCK), 0, 2) < 1).astype(jnp.int32), jax.random.fold_in(arg_keys[7], 1), 0, 1)
    return dict(tokens=tokens, grad_output=grad_output, gate_weight=gate_weight, up_weight=up_weight, down_weight=down_weight, gate_mask=gate_mask, up_mask=up_mask, down_mask=down_mask)


def expand(mask_table):
    return jnp.repeat(jnp.repeat(mask_table, BLOCK, axis=0), BLOCK, axis=1).astype(jnp.bfloat16)


def contract_rows(left, right_side):
    return lax.dot_general(left, right_side, (((0,), (0,)), ((), ())), preferred_element_type=jnp.float32)


def reference(tokens, grad_output, gate_weight, up_weight, down_weight, gate_mask, up_mask, down_mask):
    gate_keep = expand(gate_mask)
    up_keep = expand(up_mask)
    down_keep = expand(down_mask)
    gate_eff = gate_weight * gate_keep
    up_eff = up_weight * up_keep
    down_eff = down_weight * down_keep
    gate = jnp.dot(tokens, gate_eff, preferred_element_type=jnp.float32)
    up = jnp.dot(tokens, up_eff, preferred_element_type=jnp.float32)
    sigmoid_gate = jax.nn.sigmoid(gate)
    activated = gate * sigmoid_gate
    hidden = (activated * up).astype(jnp.bfloat16)
    output = jnp.dot(hidden, down_eff, preferred_element_type=jnp.float32).astype(jnp.bfloat16)
    grad_hidden = jnp.dot(grad_output, down_eff.T, preferred_element_type=jnp.float32)
    grad_gate_act = (grad_hidden * up * sigmoid_gate * (1.0 + gate * (1.0 - sigmoid_gate))).astype(jnp.bfloat16)
    grad_up_act = (grad_hidden * activated).astype(jnp.bfloat16)
    grad_gate = (gate_keep.astype(jnp.float32) * contract_rows(tokens, grad_gate_act)).astype(jnp.bfloat16)
    grad_up = (up_keep.astype(jnp.float32) * contract_rows(tokens, grad_up_act)).astype(jnp.bfloat16)
    grad_down = (down_keep.astype(jnp.float32) * contract_rows(hidden, grad_output)).astype(jnp.bfloat16)
    grad_tokens = (jnp.dot(grad_gate_act, gate_eff.T, preferred_element_type=jnp.float32)
                   + jnp.dot(grad_up_act, up_eff.T, preferred_element_type=jnp.float32)).astype(jnp.bfloat16)
    return output, grad_tokens, grad_gate, grad_up, grad_down
```

```python
import jax
import jax.numpy as jnp
from jax import lax
from jax.experimental import pallas as pl
from jax.experimental.pallas import tpu as pltpu
from jax.sharding import PartitionSpec as P

BF = jnp.bfloat16
F32 = jnp.float32
SIDE = 128
RING = 4
DEPTH = 8
PHASE_DTYPES = (BF, F32)

FAR_R, OWN_R, SUM_R, FAR_L, OWN_L, SUM_L = range(6)


def mm(left, right_side, dims):
    return lax.dot_general(left, right_side, (dims, ((), ())), preferred_element_type=F32)


def kernel(
    tok_in, cot_in, wg_in, wu_in, wd_in, gmask, umask, dmask,
    o_out, gt_out, gg_out, gu_out, gd_out,
    rows, weights, weight_d, part, sent1, got1, acc1, sent2, got2, fin,
    acts, outs, peer, zsent, zgot, grads, grad_d, small,
    ag_s, ag_r, rs_s, rs_r, av_s, av_r, ex_s, ex_r, zr_s, zr_r, loc,
):
    dp = lax.axis_index("dp")
    tensor = lax.axis_index("tensor")
    x, y = dp // RING, dp % RING
    z, core = tensor // 2, tensor % 2
    sends = []

    def wrap(value, n):
        return lax.rem(value + 2 * n, n)

    def at(dx=0, dy=0, dz=0, dc=0):
        return {
            "dp": wrap(x + dx, RING) * RING + wrap(y + dy, RING),
            "tensor": wrap(z + dz, DEPTH) * 2 + (1 - core if dc else core),
        }

    def remote(src, dst, s_sem, r_sem, device):
        return pltpu.make_async_remote_copy(
            src_ref=src, dst_ref=dst, send_sem=s_sem, recv_sem=r_sem,
            device_id=device, device_id_type=pl.DeviceIdType.MESH,
        )

    def push(src, dst, s_sem, r_sem, device):
        copy = remote(src, dst, s_sem, r_sem, device)
        copy.start()
        sends.append(copy)

    def arrived(dst, s_sem, r_sem, device):
        remote(dst, dst, s_sem, r_sem, device).wait_recv()

    def block_rows(zz, cc):
        return pl.ds(pl.multiple_of((wrap(zz, DEPTH) * 2 + cc) * 64, 64), 64)

    mine = block_rows(z, core)
    loads = [
        pltpu.make_async_copy(tok_in, rows.at[0, mine], loc.at[0]),
        pltpu.make_async_copy(cot_in, rows.at[1, mine], loc.at[1]),
        pltpu.make_async_copy(wg_in, weights.at[0], loc.at[2]),
        pltpu.make_async_copy(wu_in, weights.at[1], loc.at[3]),
        pltpu.make_async_copy(wd_in, weight_d, loc.at[4]),
    ]
    for load in loads:
        load.start()

    barrier = pltpu.get_barrier_semaphore()
    peers = [at(dx=1), at(dx=-1), at(dy=1), at(dy=-1), at(dz=1), at(dz=-1), at(dc=1)]
    for device in peers:
        pl.semaphore_signal(barrier, inc=1, device_id=device, device_id_type=pl.DeviceIdType.MESH)
    pl.semaphore_wait(barrier, len(peers))

    def half(zz, cc, second):
        start = (wrap(zz, DEPTH) * 2 + cc) * 64 + 32 * second
        return pl.ds(pl.multiple_of(start, 32), 32)

    def z_push(i, slot, where, device):
        ref = rows.at[i, where]
        push(ref, ref, ag_s.at[i, slot], ag_r.at[i, slot], device)

    def z_arrived(i, slot, where, device):
        arrived(rows.at[i, where], ag_s.at[i, slot], ag_r.at[i, slot], device)

    up, down, other = at(dz=1), at(dz=-1), at(dc=1)

    def gather_start(i):
        loads[i].wait()
        z_push(i, 0, mine, up)
        z_push(i, 4, mine, down)
        z_push(i, 8, mine, other)

    def gather_step(i, k):
        if k < 4:
            z_arrived(i, k - 1, block_rows(z - k, core), up)
            if k < 3:
                z_push(i, k, block_rows(z - k, core), up)
            else:
                z_push(i, 3, half(z - 3, core, 0), up)
            z_push(i, 8 + 2 * k - 1, block_rows(z - k, core), other)
            z_arrived(i, 4 + k - 1, block_rows(z + k, core), down)
            if k < 3:
                z_push(i, 4 + k, block_rows(z + k, core), down)
            else:
                z_push(i, 7, half(z + 3, core, 1), down)
            z_push(i, 8 + 2 * k, block_rows(z + k, core), other)
        else:
            z_arrived(i, 3, half(z - 4, core, 0), up)
            z_arrived(i, 7, half(z + 4, core, 1), down)
            z_push(i, 15, block_rows(z + 4, core), other)

    def gather_end(i):
        z_arrived(i, 8, block_rows(z, 1 - core), other)
        for k in range(1, 4):
            z_arrived(i, 8 + 2 * k - 1, block_rows(z - k, 1 - core), other)
            z_arrived(i, 8 + 2 * k, block_rows(z + k, 1 - core), other)
        z_arrived(i, 15, block_rows(z + 4, 1 - core), other)

    gather_start(0)
    gather_start(1)

    def keep(mask, i, j):
        return mask[i, j].astype(F32)

    def mask_weight(ref, mask, n_rows, n_cols):
        def body(i, carry):
            rows_i = pl.ds(pl.multiple_of(i * SIDE, SIDE), SIDE)
            for j in range(n_cols):
                cols = pl.ds(j * SIDE, SIDE)
                ref[rows_i, cols] = (ref[rows_i, cols].astype(F32) * keep(mask, i, j)).astype(BF)
            return carry

        lax.fori_loop(0, n_rows, body, 0)

    for load in loads[2:]:
        load.wait()
    mask_weight(weights.at[0], gmask, 4, 7)
    gather_step(0, 1)
    gather_step(1, 1)
    mask_weight(weights.at[1], umask, 4, 7)
    gather_step(0, 2)
    gather_step(1, 2)
    mask_weight(weight_d, dmask, 7, 4)
    gather_step(0, 3)
    gather_step(1, 3)
    gather_step(0, 4)
    gather_step(1, 4)
    gather_end(0)

    def tiles(body, count=4):
        def step(i, carry):
            body(i, pl.ds(pl.multiple_of(i * 256, 256), 256))
            return carry

        lax.fori_loop(0, count, step, 0)

    def partial(a):
        def body(i, where):
            if a < 2:
                part[a, where] = mm(rows[0, where], weights[a], ((1,), (0,)))
            else:
                part[2, where] = mm(rows[1, where], weight_d[...], ((1,), (1,)))

        tiles(body)

    def ring(h, phase):
        if (h + phase) % 2 == 0:
            return x, at(dx=1), at(dx=-1)
        return y, at(dy=1), at(dy=-1)

    def rs_refs(a, h, phase):
        if phase == 0:
            return part.at[a], h * 512, 64, sent1.at[a, h], got1.at[a, h], acc1.at[a, h]
        return acc1.at[a, h], 0, 16, sent2.at[a, h], got2.at[a, h], fin.at[a, h]

    def rs_sem(sems, a, h, phase, slot):
        return sems.at[a, h, 6 * phase + slot]

    def rs_push(a, h, phase, slot, device):
        _, _, _, sent, got, _ = rs_refs(a, h, phase)
        push(
            sent.at[slot], got.at[slot],
            rs_sem(rs_s, a, h, phase, slot), rs_sem(rs_r, a, h, phase, slot), device,
        )

    def rs_arrived(a, h, phase, slot, device):
        _, _, _, _, got, _ = rs_refs(a, h, phase)
        arrived(
            got.at[slot], rs_sem(rs_s, a, h, phase, slot), rs_sem(rs_r, a, h, phase, slot), device
        )

    def rs_block(a, h, phase, d, second):
        src, base, n, _, _, _ = rs_refs(a, h, phase)
        start = base + 2 * n * d + n * second
        return src[pl.ds(pl.multiple_of(start, n), n), :]

    def rs_first(a, h, phase):
        q, right, left = ring(h, phase)
        sent = rs_refs(a, h, phase)[3]
        dtype = PHASE_DTYPES[phase]
        far, to_r, to_l = wrap(q + 2, RING), wrap(q + 1, RING), wrap(q - 1, RING)
        for slot, d, second, device in (
            (FAR_R, far, 0, right), (FAR_L, far, 1, left), (OWN_R, to_r, 1, right), (OWN_L, to_l, 0, left),
        ):
            sent[slot] = rs_block(a, h, phase, d, second).astype(dtype)
            rs_push(a, h, phase, slot, device)

    def rs_second(a, h, phase):
        q, right, left = ring(h, phase)
        _, _, _, sent, got, _ = rs_refs(a, h, phase)
        dtype = PHASE_DTYPES[phase]
        to_r, to_l = wrap(q + 1, RING), wrap(q - 1, RING)
        rs_arrived(a, h, phase, FAR_R, right)
        sent[SUM_R] = (rs_block(a, h, phase, to_r, 0) + got[FAR_R].astype(F32)).astype(dtype)
        rs_push(a, h, phase, SUM_R, right)
        rs_arrived(a, h, phase, FAR_L, left)
        sent[SUM_L] = (rs_block(a, h, phase, to_l, 1) + got[FAR_L].astype(F32)).astype(dtype)
        rs_push(a, h, phase, SUM_L, left)

    def rs_last(a, h, phase):
        q, right, left = ring(h, phase)
        _, _, n, _, got, dst = rs_refs(a, h, phase)
        rs_arrived(a, h, phase, OWN_R, right)
        rs_arrived(a, h, phase, OWN_L, left)
        rs_arrived(a, h, phase, SUM_R, right)
        rs_arrived(a, h, phase, SUM_L, left)
        dst[pl.ds(0, n), :] = (
            rs_block(a, h, phase, q, 0) + got[SUM_R].astype(F32) + got[OWN_L].astype(F32)
        )
        dst[pl.ds(n, n), :] = (
            rs_block(a, h, phase, q, 1) + got[OWN_R].astype(F32) + got[SUM_L].astype(F32)
        )

    def both(step, a, phase):
        for h in range(2):
            step(a, h, phase)

    def av_rows(h, phase, d, second=None):
        n = 32 if phase == 0 else 128
        start = h * 512 + 128 * ring(h, 0)[0] + 32 * d if phase == 0 else h * 512 + 128 * d
        if second is None:
            return pl.ds(pl.multiple_of(start, n), n)
        return pl.ds(pl.multiple_of(start + n // 2 * second, n // 2), n // 2)

    def av_move(a, h, phase, slot, where, device, send):
        ref = acts.at[a, where]
        sems = av_s.at[a, h, 4 * phase + slot], av_r.at[a, h, 4 * phase + slot]
        if send:
            push(ref, ref, *sems, device)
        else:
            arrived(ref, *sems, device)

    def av_first(a, h, phase):
        q, right, left = ring(h, 1 - phase)
        av_move(a, h, phase, 0, av_rows(h, phase, q), right, True)
        av_move(a, h, phase, 1, av_rows(h, phase, q), left, True)

    def av_second(a, h, phase):
        q, right, left = ring(h, 1 - phase)
        from_l, from_r = wrap(q - 1, RING), wrap(q + 1, RING)
        av_move(a, h, phase, 0, av_rows(h, phase, from_l), right, False)
        av_move(a, h, phase, 2, av_rows(h, phase, from_l, 0), right, True)
        av_move(a, h, phase, 1, av_rows(h, phase, from_r), left, False)
        av_move(a, h, phase, 3, av_rows(h, phase, from_r, 1), left, True)

    def av_last(a, h, phase):
        q, right, left = ring(h, 1 - phase)
        far = wrap(q + 2, RING)
        av_move(a, h, phase, 2, av_rows(h, phase, far, 0), right, False)
        av_move(a, h, phase, 3, av_rows(h, phase, far, 1), left, False)

    def own_rows(h):
        return av_rows(h, 0, ring(h, 1)[0])

    def exchange(b):
        push(outs.at[b, :, 1 - core], peer.at[b], ex_s.at[b], ex_r.at[b], other)

    def exchanged(b):
        arrived(peer.at[b], ex_s.at[b], ex_r.at[b], other)

    def chip_sum(b, zz):
        return outs[b, wrap(zz, DEPTH), core] + peer[b, wrap(zz, DEPTH)]

    def zr_move(b, way, k, send):
        where = pl.ds(0, 64) if k < 4 else pl.ds(32 * way, 32)
        sems = zr_s.at[b, way, k - 1], zr_r.at[b, way, k - 1]
        device = (up, down)[way]
        if send:
            push(zsent.at[b, way, k - 1, where], zgot.at[b, way, k - 1, where], *sems, device)
        else:
            arrived(zgot.at[b, way, k - 1, where], *sems, device)

    def zr_step(b, k):
        for way in range(2):
            target = z + k if way == 0 else z - k
            if k == 4:
                where = pl.ds(32 * way, 32)
                wrapped = wrap(target, DEPTH)
                zsent[b, way, 3, where] = outs[b, wrapped, core, where] + peer[b, wrapped, where]
            else:
                zr_move(b, way, k + 1, False)
                total = chip_sum(b, target)
                if k == 3:
                    fresh, rest = pl.ds(32 * way, 32), pl.ds(32 - 32 * way, 32)
                    zsent[b, way, 2] = total
                    zsent[b, way, 2, fresh] = zsent[b, way, 2, fresh] + zgot[b, way, 3, fresh]
                else:
                    zsent[b, way, k - 1] = total + zgot[b, way, k]
            zr_move(b, way, k, True)

    def zr_last(b, out):
        zr_move(b, 0, 1, False)
        zr_move(b, 1, 1, False)
        small[b] = (chip_sum(b, z) + zgot[b, 0, 0] + zgot[b, 1, 0]).astype(BF)
        pltpu.make_async_copy(small.at[b], out, loc.at[5 + b]).start()

    def store(out, src, i):
        pltpu.make_async_copy(src, out, loc.at[i]).start()

    def grad_weights():
        def body(i, where):
            left = rows[0, :, where].T
            for a, mask in ((0, gmask), (1, umask)):
                tile = mm(left, acts[1 + a], ((1,), (0,)))
                for r in range(2):
                    for j in range(7):
                        cols = slice(j * SIDE, (j + 1) * SIDE)
                        out_rows = pl.ds(pl.multiple_of(i * 256 + r * SIDE, SIDE), SIDE)
                        grads[a, out_rows, cols] = (
                            tile[r * SIDE : (r + 1) * SIDE, cols] * keep(mask, 2 * i + r, j)
                        ).astype(BF)

        tiles(body, 2)

    def grad_down():
        def step(i, carry):
            where = pl.ds(pl.multiple_of(i * SIDE, SIDE), SIDE)
            tile = mm(acts[0, :, where].T, rows[1], ((1,), (0,)))
            for j in range(4):
                cols = slice(j * SIDE, (j + 1) * SIDE)
                grad_d[where, cols] = (tile[:, cols] * keep(dmask, i, j)).astype(BF)
            return carry

        lax.fori_loop(0, 7, step, 0)

    partial(0)
    both(rs_first, 0, 0)
    partial(1)
    both(rs_first, 1, 0)
    gather_end(1)
    partial(2)
    both(rs_second, 0, 0)
    both(rs_first, 2, 0)
    both(rs_second, 1, 0)
    both(rs_last, 0, 0)
    both(rs_first, 0, 1)
    both(rs_second, 2, 0)
    both(rs_last, 1, 0)
    both(rs_first, 1, 1)
    both(rs_second, 0, 1)
    both(rs_second, 1, 1)
    both(rs_last, 2, 0)
    both(rs_first, 2, 1)
    both(rs_last, 0, 1)
    both(rs_last, 1, 1)
    for h in range(2):
        gate = fin[0, h]
        acts[0, own_rows(h)] = (gate * jax.nn.sigmoid(gate) * fin[1, h]).astype(BF)
        av_first(0, h, 0)
    both(rs_second, 2, 1)
    both(av_second, 0, 0)
    both(rs_last, 2, 1)
    for h in range(2):
        gate, upv, grad = fin[0, h], fin[1, h], fin[2, h]
        s = jax.nn.sigmoid(gate)
        acts[1, own_rows(h)] = (grad * upv * s * (1.0 + gate * (1.0 - s))).astype(BF)
        acts[2, own_rows(h)] = (grad * (gate * s)).astype(BF)
        av_first(1, h, 0)
        av_first(2, h, 0)
    both(av_last, 0, 0)
    both(av_first, 0, 1)
    both(av_second, 1, 0)
    both(av_second, 2, 0)
    both(av_last, 1, 0)
    both(av_first, 1, 1)
    both(av_second, 0, 1)
    both(av_last, 2, 0)
    both(av_first, 2, 1)
    both(av_last, 0, 1)

    def output_part(i, where):
        tile = mm(acts[0, where], weight_d[...], ((1,), (0,)))
        outs[0, pl.ds(2 * i, 2)] = tile.reshape(2, 2, 64, 512)

    tiles(output_part)
    exchange(0)
    both(av_second, 1, 1)
    exchanged(0)
    zr_step(0, 4)
    both(av_second, 2, 1)
    zr_step(0, 3)
    both(av_last, 1, 1)
    zr_step(0, 2)
    grad_down()
    store(gd_out, grad_d, 7)
    zr_step(0, 1)
    both(av_last, 2, 1)

    def tokens_part(i, where):
        tile = mm(acts[1, where], weights[0], ((1,), (1,))) + mm(acts[2, where], weights[1], ((1,), (1,)))
        outs[1, pl.ds(2 * i, 2)] = tile.reshape(2, 2, 64, 512)

    tiles(tokens_part)
    exchange(1)
    zr_last(0, o_out)
    exchanged(1)
    zr_step(1, 4)
    grad_weights()
    store(gg_out, grads.at[0], 8)
    store(gu_out, grads.at[1], 9)
    zr_step(1, 3)
    zr_step(1, 2)
    zr_step(1, 1)
    zr_last(1, gt_out)

    pltpu.make_async_copy(small.at[0], o_out, loc.at[5]).wait()
    pltpu.make_async_copy(small.at[1], gt_out, loc.at[6]).wait()
    pltpu.make_async_copy(grad_d, gd_out, loc.at[7]).wait()
    pltpu.make_async_copy(grads.at[0], gg_out, loc.at[8]).wait()
    pltpu.make_async_copy(grads.at[1], gu_out, loc.at[9]).wait()
    for copy in sends:
        copy.wait_send()


def shards(*args):
    anywhere = pl.BlockSpec(memory_space=pl.ANY)
    scalars = pl.BlockSpec(memory_space=pltpu.SMEM)
    dma = pltpu.SemaphoreType.DMA
    d1, d2 = PHASE_DTYPES
    return tuple(
        pl.pallas_call(
            kernel,
            out_shape=[
                jax.ShapeDtypeStruct((64, 512), BF),
                jax.ShapeDtypeStruct((64, 512), BF),
                jax.ShapeDtypeStruct((512, 896), BF),
                jax.ShapeDtypeStruct((512, 896), BF),
                jax.ShapeDtypeStruct((896, 512), BF),
            ],
            in_specs=[anywhere] * 5 + [scalars] * 3,
            out_specs=[anywhere] * 5,
            scratch_shapes=[
                pltpu.VMEM((2, 1024, 512), BF),
                pltpu.VMEM((2, 512, 896), BF),
                pltpu.VMEM((896, 512), BF),
                pltpu.VMEM((3, 1024, 896), F32),
                pltpu.VMEM((3, 2, 6, 64, 896), d1),
                pltpu.VMEM((3, 2, 6, 64, 896), d1),
                pltpu.VMEM((3, 2, 128, 896), F32),
                pltpu.VMEM((3, 2, 6, 16, 896), d2),
                pltpu.VMEM((3, 2, 6, 16, 896), d2),
                pltpu.VMEM((3, 2, 32, 896), F32),
                pltpu.VMEM((3, 1024, 896), BF),
                pltpu.VMEM((2, 8, 2, 64, 512), F32),
                pltpu.VMEM((2, 8, 64, 512), F32),
                pltpu.VMEM((2, 2, 4, 64, 512), F32),
                pltpu.VMEM((2, 2, 4, 64, 512), F32),
                pltpu.VMEM((2, 512, 896), BF),
                pltpu.VMEM((896, 512), BF),
                pltpu.VMEM((2, 64, 512), BF),
                dma((2, 16)), dma((2, 16)),
                dma((3, 2, 12)), dma((3, 2, 12)),
                dma((3, 2, 8)), dma((3, 2, 8)),
                dma((2,)), dma((2,)),
                dma((2, 2, 4)), dma((2, 2, 4)),
                dma((10,)),
            ],
            compiler_params=pltpu.CompilerParams(
                collective_id=0, has_side_effects=True, vmem_limit_bytes=64_000_000
            ),
            name="ffn",
        )(*args)
    )


def solution(mesh):
    return jax.shard_map(
        shards,
        mesh=mesh,
        in_specs=(
            P("tensor", "dp"),
            P("tensor", "dp"),
            P("dp", "tensor"),
            P("dp", "tensor"),
            P("tensor", "dp"),
            P("dp", "tensor"),
            P("dp", "tensor"),
            P("tensor", "dp"),
        ),
        out_specs=(
            P("tensor", "dp"),
            P("tensor", "dp"),
            P("dp", "tensor"),
            P("dp", "tensor"),
            P("tensor", "dp"),
        ),
        check_vma=False,
    )
```

```python
import jax
import jax.numpy as jnp
from jax import lax
from jax.experimental import pallas as pl
from jax.experimental.pallas import tpu as pltpu
from jax.sharding import PartitionSpec as P

BF = jnp.bfloat16
F32 = jnp.float32
SIDE = 128
RING = 4
DEPTH = 8
CHUNKS = 2
OWN = 64 // CHUNKS
MANY = 1024 // CHUNKS
PIECE = 256
PHASE_DTYPES = (BF, F32)

FAR_R, OWN_R, SUM_R, FAR_L, OWN_L, SUM_L = range(6)

SCHEDULE = (
    ("G", 0, 0),
    ("G", 1, 0),
    ("M", 1),
    ("M", 0),
    ("M", 2),
    ("N", 0, 0, 1),
    ("N", 0, 0, 7),
    ("N", 0, 0, 2),
    ("N", 0, 0, 6),
    ("N", 1, 0, 1),
    ("N", 1, 0, 7),
    ("N", 1, 0, 2),
    ("N", 1, 0, 6),
    ("G", 0, 1),
    ("N", 0, 0, 3),
    ("N", 0, 0, 5),
    ("N", 0, 0, 4),
    ("E", 0, 0),
    ("P", 0, 0),
    ("F", 0, 0, 0, 0),
    ("N", 1, 0, 3),
    ("N", 1, 0, 5),
    ("F", 0, 0, 1, 0),
    ("N", 1, 0, 4),
    ("P", 1, 0),
    ("F", 1, 0, 0, 0),
    ("F", 1, 0, 1, 0),
    ("N", 0, 1, 1),
    ("N", 0, 1, 7),
    ("N", 0, 1, 2),
    ("N", 0, 1, 6),
    ("G", 1, 1),
    ("E", 1, 0),
    ("P", 2, 0),
    ("F", 2, 0, 0, 0),
    ("F", 2, 0, 1, 0),
    ("S", 0, 0, 0, 0),
    ("S", 0, 0, 1, 0),
    ("S", 1, 0, 0, 0),
    ("N", 0, 1, 3),
    ("N", 0, 1, 5),
    ("S", 1, 0, 1, 0),
    ("N", 0, 1, 4),
    ("E", 0, 1),
    ("P", 0, 1),
    ("N", 1, 1, 1),
    ("N", 1, 1, 2),
    ("N", 1, 1, 6),
    ("F", 0, 1, 0, 0),
    ("F", 0, 1, 1, 0),
    ("N", 1, 1, 7),
    ("S", 2, 0, 0, 0),
    ("S", 2, 0, 1, 0),
    ("P", 1, 1),
    ("F", 1, 1, 0, 0),
    ("F", 1, 1, 1, 0),
    ("L", 0, 0, 0, 0),
    ("F", 0, 0, 0, 1),
    ("L", 0, 0, 1, 0),
    ("F", 0, 0, 1, 1),
    ("L", 1, 0, 0, 0),
    ("F", 1, 0, 0, 1),
    ("L", 1, 0, 1, 0),
    ("F", 1, 0, 1, 1),
    ("S", 0, 1, 0, 0),
    ("S", 0, 1, 1, 0),
    ("N", 1, 1, 3),
    ("N", 1, 1, 4),
    ("N", 1, 1, 5),
    ("L", 2, 0, 0, 0),
    ("F", 2, 0, 0, 1),
    ("E", 1, 1),
    ("L", 2, 0, 1, 0),
    ("F", 2, 0, 1, 1),
    ("P", 2, 1),
    ("F", 2, 1, 0, 0),
    ("F", 2, 1, 1, 0),
    ("S", 1, 1, 0, 0),
    ("S", 1, 1, 1, 0),
    ("S", 0, 0, 1, 1),
    ("S", 0, 0, 0, 1),
    ("S", 1, 0, 1, 1),
    ("S", 1, 0, 0, 1),
    ("L", 0, 1, 0, 0),
    ("F", 0, 1, 0, 1),
    ("L", 0, 1, 1, 0),
    ("F", 0, 1, 1, 1),
    ("S", 2, 0, 1, 1),
    ("S", 2, 0, 0, 1),
    ("S", 2, 1, 0, 0),
    ("S", 2, 1, 1, 0),
    ("L", 1, 1, 0, 0),
    ("F", 1, 1, 0, 1),
    ("L", 1, 1, 1, 0),
    ("F", 1, 1, 1, 1),
    ("L", 0, 0, 1, 1),
    ("L", 0, 0, 0, 1),
    ("L", 1, 0, 1, 1),
    ("H", 0, 1),
    ("L", 1, 0, 0, 1),
    ("H", 0, 0),
    ("S", 0, 1, 1, 1),
    ("S", 0, 1, 0, 1),
    ("L", 2, 0, 1, 1),
    ("Q", 0, 1),
    ("L", 2, 0, 0, 1),
    ("Q", 0, 0),
    ("L", 2, 1, 0, 0),
    ("F", 2, 1, 0, 1),
    ("L", 2, 1, 1, 0),
    ("F", 2, 1, 1, 1),
    ("S", 1, 1, 1, 1),
    ("S", 1, 1, 0, 1),
    ("B", 0, 0, 1, 0),
    ("B", 0, 0, 0, 0),
    ("L", 0, 1, 1, 1),
    ("L", 0, 1, 0, 1),
    ("B", 1, 0, 1, 0),
    ("B", 1, 0, 0, 0),
    ("B", 2, 0, 1, 0),
    ("B", 2, 0, 0, 0),
    ("S", 2, 1, 1, 1),
    ("S", 2, 1, 0, 1),
    ("L", 1, 1, 1, 1),
    ("H", 1, 1),
    ("L", 1, 1, 0, 1),
    ("H", 1, 0),
    ("C", 0, 0, 1, 0),
    ("A", 0, 0, 1, 1),
    ("C", 0, 0, 0, 0),
    ("A", 0, 0, 0, 1),
    ("C", 1, 0, 1, 0),
    ("A", 1, 0, 1, 1),
    ("C", 1, 0, 0, 0),
    ("A", 1, 0, 0, 1),
    ("C", 2, 0, 1, 0),
    ("A", 2, 0, 1, 1),
    ("C", 2, 0, 0, 0),
    ("A", 2, 0, 0, 1),
    ("L", 2, 1, 1, 1),
    ("Q", 1, 1),
    ("L", 2, 1, 0, 1),
    ("Q", 1, 0),
    ("B", 0, 1, 1, 0),
    ("B", 0, 1, 0, 0),
    ("B", 0, 0, 0, 1),
    ("B", 0, 0, 1, 1),
    ("B", 1, 0, 0, 1),
    ("B", 1, 0, 1, 1),
    ("B", 2, 0, 0, 1),
    ("B", 2, 0, 1, 1),
    ("B", 1, 1, 1, 0),
    ("B", 1, 1, 0, 0),
    ("B", 2, 1, 1, 0),
    ("B", 2, 1, 0, 0),
    ("C", 0, 1, 1, 0),
    ("A", 0, 1, 1, 1),
    ("C", 0, 1, 0, 0),
    ("A", 0, 1, 0, 1),
    ("C", 0, 0, 0, 1),
    ("C", 0, 0, 1, 1),
    ("T", 0, 0, 0, 0),
    ("T", 0, 0, 0, 1),
    ("C", 1, 0, 0, 1),
    ("C", 1, 0, 1, 1),
    ("T", 1, 1, 0, 0),
    ("T", 1, 1, 0, 1),
    ("C", 2, 0, 0, 1),
    ("C", 1, 1, 1, 0),
    ("A", 1, 1, 1, 1),
    ("Z", 0, 0, 0, 4),
    ("C", 1, 1, 0, 0),
    ("A", 1, 1, 0, 1),
    ("C", 2, 0, 1, 1),
    ("T", 1, 2, 0, 0),
    ("T", 1, 2, 0, 1),
    ("C", 2, 1, 1, 0),
    ("A", 2, 1, 1, 1),
    ("C", 2, 1, 0, 0),
    ("A", 2, 1, 0, 1),
    ("Z", 0, 0, 1, 4),
    ("Z", 1, 0, 0, 4),
    ("B", 0, 1, 0, 1),
    ("B", 0, 1, 1, 1),
    ("Z", 1, 0, 1, 4),
    ("Z", 0, 0, 0, 3),
    ("Z", 0, 0, 1, 3),
    ("B", 1, 1, 1, 1),
    ("B", 1, 1, 0, 1),
    ("Z", 1, 0, 0, 3),
    ("Z", 1, 0, 1, 3),
    ("B", 2, 1, 1, 1),
    ("Z", 0, 0, 0, 2),
    ("B", 2, 1, 0, 1),
    ("Z", 0, 0, 1, 2),
    ("C", 0, 1, 1, 1),
    ("C", 0, 1, 0, 1),
    ("T", 0, 0, 1, 0),
    ("T", 0, 0, 1, 1),
    ("D", 0),
    ("Z", 1, 0, 0, 2),
    ("C", 1, 1, 1, 1),
    ("D", 1),
    ("C", 1, 1, 0, 1),
    ("T", 1, 1, 1, 0),
    ("T", 1, 1, 1, 1),
    ("W", 0, 1),
    ("Z", 0, 0, 0, 1),
    ("Z", 0, 1, 0, 4),
    ("Z", 1, 0, 1, 2),
    ("W", 0, 0),
    ("Z", 0, 0, 1, 1),
    ("C", 2, 1, 0, 1),
    ("C", 2, 1, 1, 1),
    ("T", 1, 2, 1, 0),
    ("T", 1, 2, 1, 1),
    ("W", 1, 0),
    ("W", 1, 1),
    ("Z", 0, 1, 1, 4),
    ("D", 2),
    ("Z", 1, 0, 0, 1),
    ("D", 3),
    ("Z", 1, 1, 0, 4),
    ("Y", 0, 0, 0),
    ("Z", 1, 1, 1, 4),
    ("Z", 0, 1, 0, 3),
    ("Z", 1, 0, 1, 1),
    ("Y", 0, 0, 1),
    ("Z", 0, 1, 1, 3),
    ("Y", 1, 0, 0),
    ("Z", 1, 1, 0, 3),
    ("Z", 1, 1, 1, 3),
    ("Z", 0, 1, 0, 2),
    ("Y", 1, 0, 1),
    ("Z", 0, 1, 1, 2),
    ("Z", 1, 1, 0, 2),
    ("Z", 1, 1, 1, 2),
    ("Z", 0, 1, 0, 1),
    ("Z", 0, 1, 1, 1),
    ("Z", 1, 1, 0, 1),
    ("Z", 1, 1, 1, 1),
    ("Y", 0, 1, 0),
    ("Y", 0, 1, 1),
    ("Y", 1, 1, 0),
    ("Y", 1, 1, 1),
)


def mm(left, right_side, dims):
    return lax.dot_general(left, right_side, (dims, ((), ())), preferred_element_type=F32)


def kernel(
    tok_in, cot_in, wg_in, wu_in, wd_in, gm_in, um_in, dm_in,
    o_out, gt_out, gg_out, gu_out, gd_out,
    rows, weights, weight_d, part, sent1, got1, acc1, sent2, got2, fin,
    acts, outs, peer, zsent, zgot, gmask, umask, dmask,
    ag_s, ag_r, rs_s, rs_r, av_s, av_r, ex_s, ex_r, zr_s, zr_r, loc,
):
    dp = lax.axis_index("dp")
    tensor = lax.axis_index("tensor")
    x, y = dp // RING, dp % RING
    z, core = tensor // 2, tensor % 2
    sends = []

    def wrap(value, n):
        return lax.rem(value + 2 * n, n)

    def at(dx=0, dy=0, dz=0, dc=0):
        return {
            "dp": wrap(x + dx, RING) * RING + wrap(y + dy, RING),
            "tensor": wrap(z + dz, DEPTH) * 2 + (1 - core if dc else core),
        }

    def remote(src, dst, s_sem, r_sem, device):
        return pltpu.make_async_remote_copy(
            src_ref=src, dst_ref=dst, send_sem=s_sem, recv_sem=r_sem,
            device_id=device, device_id_type=pl.DeviceIdType.MESH,
        )

    def push(src, dst, s_sem, r_sem, device):
        copy = remote(src, dst, s_sem, r_sem, device)
        copy.start()
        sends.append(copy)

    def arrived(dst, s_sem, r_sem, device):
        remote(dst, dst, s_sem, r_sem, device).wait_recv()

    def block_rows(zz, cc):
        return pl.ds(pl.multiple_of((wrap(zz, DEPTH) * 2 + cc) * OWN, OWN), OWN)

    mine, mine_there = block_rows(z, core), block_rows(z, 1 - core)
    row_loads = [
        [
            pltpu.make_async_copy(
                ref.at[pl.ds(OWN * k, OWN)], rows.at[i, k, mine], loc.at[CHUNKS * i + k]
            )
            for k in range(CHUNKS)
        ]
        for i, ref in enumerate((tok_in, cot_in))
    ]
    other_loads = [
        pltpu.make_async_copy(src, dst, loc.at[2 * CHUNKS + n])
        for n, (src, dst) in enumerate(
            (
                (gm_in, gmask), (um_in, umask), (dm_in, dmask),
                (wg_in, weights.at[0]), (wu_in, weights.at[1]), (wd_in, weight_d),
            )
        )
    ]
    for load in row_loads[0] + row_loads[1] + other_loads:
        load.start()

    barrier = pltpu.get_barrier_semaphore()
    peers = [at(dx=1), at(dx=-1), at(dy=1), at(dy=-1), at(dc=1)]
    peers += [at(dz=d) for d in (1, -1, 2, -2)]
    for device in peers:
        pl.semaphore_signal(barrier, inc=1, device_id=device, device_id_type=pl.DeviceIdType.MESH)
    pl.semaphore_wait(barrier, len(peers))

    def z_push(i, k, slot, where, device):
        ref = rows.at[i, k, where]
        push(ref, ref, ag_s.at[i, k, slot], ag_r.at[i, k, slot], device)

    def z_arrived(i, k, slot, where, device):
        arrived(rows.at[i, k, where], ag_s.at[i, k, slot], ag_r.at[i, k, slot], device)

    up, down, other = at(dz=1), at(dz=-1), at(dc=1)

    def half(zz, second):
        start = (wrap(zz, DEPTH) * 2 + core) * OWN + OWN // 2 * second
        return pl.ds(pl.multiple_of(start, OWN // 2), OWN // 2)

    def gather_start(i, k):
        row_loads[i][k].wait()
        z_push(i, k, 8, mine, other)
        for d in (2, -2, 1, -1):
            z_push(i, k, d % DEPTH, mine, at(dz=d))

    def gather_step(i, k, d):
        if d == 4:
            z_arrived(i, k, 4, half(z - 4, 0), up)
            z_arrived(i, k, 0, half(z - 4, 1), up)
            z_push(i, k, 12, block_rows(z - 4, core), other)
            return
        n = d if d < 4 else d - DEPTH
        sign = 1 if n > 0 else -1
        z_arrived(i, k, d, block_rows(z - n, core), up)
        if n == sign:
            z_push(i, k, 3 * sign % DEPTH, block_rows(z - n, core), at(dz=2 * sign))
        elif n == 2 * sign:
            z_push(i, k, 4 if n > 0 else 0, half(z - n, 0 if n > 0 else 1), at(dz=2 * sign))
        z_push(i, k, 8 + d, block_rows(z - n, core), other)

    def gather_end(i, k):
        z_arrived(i, k, 8, mine_there, other)
        for d in range(1, DEPTH):
            z_arrived(i, k, 8 + d, block_rows(z - d, 1 - core), other)

    def keep(mask, i, j):
        return mask[i, j].astype(F32)

    def mask_weight(n):
        for load in (other_loads[n], other_loads[3 + n]):
            load.wait()
        ref = weight_d if n == 2 else weights.at[n]
        n_rows, n_cols = (7, 4) if n == 2 else (4, 7)

        def body(i, carry):
            rows_i = pl.ds(pl.multiple_of(i * SIDE, SIDE), SIDE)
            for j in range(n_cols):
                cols = pl.ds(j * SIDE, SIDE)
                factor = keep(dmask, j, i) if n == 2 else keep((gmask, umask)[n], i, j)
                ref[rows_i, cols] = (ref[rows_i, cols].astype(F32) * factor).astype(BF)
            return carry

        lax.fori_loop(0, n_rows, body, 0)

    def tiles(body):
        def step(i, carry):
            body(i, pl.ds(pl.multiple_of(i * 256, 256), 256))
            return carry

        lax.fori_loop(0, MANY // 256, step, 0)

    def partial(a, k):
        def body(i, where):
            if a < 2:
                part[a, k, where] = mm(rows[0, k, where], weights[a], ((1,), (0,)))
            else:
                part[2, k, where] = mm(rows[1, k, where], weight_d[...], ((1,), (1,)))

        tiles(body)

    def ring(h, phase):
        if (h + phase) % 2 == 0:
            return x, at(dx=1), at(dx=-1)
        return y, at(dy=1), at(dy=-1)

    def rs_refs(a, k, h, phase):
        if phase == 0:
            return (
                part.at[a, k], h * (MANY // 2), MANY // 16,
                sent1.at[a, k, h], got1.at[a, k, h], acc1.at[a, k, h],
            )
        return acc1.at[a, k, h], 0, MANY // 64, sent2.at[a, k, h], got2.at[a, k, h], fin.at[a, k, h]

    def rs_sems(a, k, h, phase, slot):
        return rs_s.at[a, k, h, 6 * phase + slot], rs_r.at[a, k, h, 6 * phase + slot]

    def rs_push(a, k, h, phase, slot, device):
        _, _, _, sent, got, _ = rs_refs(a, k, h, phase)
        push(sent.at[slot], got.at[slot], *rs_sems(a, k, h, phase, slot), device)

    def rs_arrived(a, k, h, phase, slot, device):
        got = rs_refs(a, k, h, phase)[4]
        arrived(got.at[slot], *rs_sems(a, k, h, phase, slot), device)

    def rs_block(a, k, h, phase, d, second):
        src, base, n, _, _, _ = rs_refs(a, k, h, phase)
        start = base + 2 * n * d + n * second
        return src[pl.ds(pl.multiple_of(start, n), n), :]

    def rs_first(a, k, h, phase):
        q, right, left = ring(h, phase)
        sent = rs_refs(a, k, h, phase)[3]
        dtype = PHASE_DTYPES[phase]
        far, to_r, to_l = wrap(q + 2, RING), wrap(q + 1, RING), wrap(q - 1, RING)
        for slot, d, second, device in (
            (FAR_R, far, 0, right), (FAR_L, far, 1, left), (OWN_R, to_r, 1, right), (OWN_L, to_l, 0, left),
        ):
            sent[slot] = rs_block(a, k, h, phase, d, second).astype(dtype)
            rs_push(a, k, h, phase, slot, device)

    def rs_second(a, k, h, phase):
        q, right, left = ring(h, phase)
        _, _, _, sent, got, _ = rs_refs(a, k, h, phase)
        dtype = PHASE_DTYPES[phase]
        to_r, to_l = wrap(q + 1, RING), wrap(q - 1, RING)
        rs_arrived(a, k, h, phase, FAR_R, right)
        sent[SUM_R] = (rs_block(a, k, h, phase, to_r, 0) + got[FAR_R].astype(F32)).astype(dtype)
        rs_push(a, k, h, phase, SUM_R, right)
        rs_arrived(a, k, h, phase, FAR_L, left)
        sent[SUM_L] = (rs_block(a, k, h, phase, to_l, 1) + got[FAR_L].astype(F32)).astype(dtype)
        rs_push(a, k, h, phase, SUM_L, left)

    def rs_last(a, k, h, phase):
        q, right, left = ring(h, phase)
        _, _, n, _, got, dst = rs_refs(a, k, h, phase)
        rs_arrived(a, k, h, phase, OWN_R, right)
        rs_arrived(a, k, h, phase, OWN_L, left)
        rs_arrived(a, k, h, phase, SUM_R, right)
        rs_arrived(a, k, h, phase, SUM_L, left)
        dst[pl.ds(0, n), :] = (
            rs_block(a, k, h, phase, q, 0) + got[SUM_R].astype(F32) + got[OWN_L].astype(F32)
        )
        dst[pl.ds(n, n), :] = (
            rs_block(a, k, h, phase, q, 1) + got[OWN_R].astype(F32) + got[SUM_L].astype(F32)
        )

    def av_rows(h, phase, d, second=None):
        n = MANY // 32 if phase == 0 else MANY // 8
        start = h * (MANY // 2) + n * d
        if phase == 0:
            start = start + MANY // 8 * ring(h, 0)[0]
        if second is None:
            return pl.ds(pl.multiple_of(start, n), n)
        return pl.ds(pl.multiple_of(start + n // 2 * second, n // 2), n // 2)

    def av_move(a, k, h, phase, slot, where, device, send):
        ref = acts.at[a, k, where]
        sems = av_s.at[a, k, h, 4 * phase + slot], av_r.at[a, k, h, 4 * phase + slot]
        if send:
            push(ref, ref, *sems, device)
        else:
            arrived(ref, *sems, device)

    def av_first(a, k, h, phase):
        q, right, left = ring(h, 1 - phase)
        av_move(a, k, h, phase, 0, av_rows(h, phase, q), right, True)
        av_move(a, k, h, phase, 1, av_rows(h, phase, q), left, True)

    def far_parts(a, k, h, phase):
        if phase == 0:
            return (None, False) if (a + k + h) % 2 == 0 else (False, None)
        return 0, 1

    def av_second(a, k, h, phase):
        q, right, left = ring(h, 1 - phase)
        from_l, from_r = wrap(q - 1, RING), wrap(q + 1, RING)
        by_r, by_l = far_parts(a, k, h, phase)
        av_move(a, k, h, phase, 0, av_rows(h, phase, from_l), right, False)
        if by_r is not False:
            av_move(a, k, h, phase, 2, av_rows(h, phase, from_l, by_r), right, True)
        av_move(a, k, h, phase, 1, av_rows(h, phase, from_r), left, False)
        if by_l is not False:
            av_move(a, k, h, phase, 3, av_rows(h, phase, from_r, by_l), left, True)

    def av_last(a, k, h, phase):
        q, right, left = ring(h, 1 - phase)
        far = wrap(q + 2, RING)
        by_r, by_l = far_parts(a, k, h, phase)
        if by_r is not False:
            av_move(a, k, h, phase, 2, av_rows(h, phase, far, by_r), right, False)
        if by_l is not False:
            av_move(a, k, h, phase, 3, av_rows(h, phase, far, by_l), left, False)

    def own_rows(h):
        return av_rows(h, 0, ring(h, 1)[0])

    def hidden(k, h):
        gate = fin[0, k, h]
        acts[0, k, own_rows(h)] = (gate * jax.nn.sigmoid(gate) * fin[1, k, h]).astype(BF)
        av_first(0, k, h, 0)

    def act_grads(k, h):
        gate, upv, grad = fin[0, k, h], fin[1, k, h], fin[2, k, h]
        s = jax.nn.sigmoid(gate)
        acts[1, k, own_rows(h)] = (grad * upv * s * (1.0 + gate * (1.0 - s))).astype(BF)
        av_first(1, k, h, 0)
        acts[2, k, own_rows(h)] = (grad * (gate * s)).astype(BF)
        av_first(2, k, h, 0)

    def feature_part(b, a, k, c):
        cols = pl.ds(c * PIECE, PIECE)
        n = 256 // (2 * OWN)

        def body(i, where):
            if a == 0:
                tile = mm(acts[0, k, where], weight_d[:, cols], ((1,), (0,)))
            else:
                tile = mm(acts[a, k, where], weights[a - 1, cols, :], ((1,), (1,)))
            tile = tile.reshape(n, 2, OWN, PIECE)
            if a == 2:
                tile = tile + outs[b, k, c, pl.ds(n * i, n)]
            outs[b, k, c, pl.ds(n * i, n)] = tile

        tiles(body)
        if a != 1:
            push(outs.at[b, k, c, :, 1 - core], peer.at[b, k, c], ex_s.at[b, k, c], ex_r.at[b, k, c], other)

    def zr_move(b, k, c, way, n, send):
        where = pl.ds(0, OWN) if n < 4 else pl.ds(OWN // 2 * way, OWN // 2)
        sems = zr_s.at[b, k, c, way, n - 1], zr_r.at[b, k, c, way, n - 1]
        device = (up, down)[way]
        got = zgot.at[b, k, c, way, n - 1, where]
        if send:
            push(zsent.at[b, k, c, way, n - 1, where], got, *sems, device)
        else:
            arrived(got, *sems, device)

    def zr_step(b, k, c, n):
        if n == 4:
            arrived(peer.at[b, k, c], ex_s.at[b, k, c], ex_r.at[b, k, c], other)
        for way in range(2):
            target = wrap(z + n if way == 0 else z - n, DEPTH)
            if n == 4:
                where = pl.ds(OWN // 2 * way, OWN // 2)
                zsent[b, k, c, way, 3, where] = (
                    outs[b, k, c, target, core, where] + peer[b, k, c, target, where]
                )
            else:
                zr_move(b, k, c, way, n + 1, False)
                if n == 3:
                    fresh, rest = pl.ds(OWN // 2 * way, OWN // 2), pl.ds(OWN // 2 * (1 - way), OWN // 2)
                    zsent[b, k, c, way, 2, rest] = (
                        outs[b, k, c, target, core, rest] + peer[b, k, c, target, rest]
                    )
                    zsent[b, k, c, way, 2, fresh] = (
                        outs[b, k, c, target, core, fresh] + peer[b, k, c, target, fresh]
                        + zgot[b, k, c, way, 3, fresh]
                    )
                else:
                    zsent[b, k, c, way, n - 1] = (
                        outs[b, k, c, target, core] + peer[b, k, c, target] + zgot[b, k, c, way, n]
                    )
            zr_move(b, k, c, way, n, True)

    def zr_last(b, k, c):
        zr_move(b, k, c, 0, 1, False)
        zr_move(b, k, c, 1, 1, False)
        total = outs[b, k, c, z, core] + peer[b, k, c, z] + zgot[b, k, c, 0, 0] + zgot[b, k, c, 1, 0]
        (o_out, gt_out)[b][pl.ds(OWN * k, OWN), pl.ds(c * PIECE, PIECE)] = total.astype(BF)

    def over_tokens(left, right_side):
        total = mm(left(0).T, right_side(0), ((1,), (0,)))
        for k in range(1, CHUNKS):
            total = total + mm(left(k).T, right_side(k), ((1,), (0,)))
        return total

    def masked_store(out, mask, total, row, flip):
        for r in range(total.shape[0] // SIDE):
            for j in range(total.shape[1] // SIDE):
                factor = keep(mask, j, row + r) if flip else keep(mask, row + r, j)
                out[pl.ds((row + r) * SIDE, SIDE), pl.ds(j * SIDE, SIDE)] = (
                    total[r * SIDE : (r + 1) * SIDE, j * SIDE : (j + 1) * SIDE] * factor
                ).astype(BF)

    def grad_weight(a, i):
        cols = pl.ds(256 * i, 256)
        total = over_tokens(lambda k: rows[0, k, :, cols], lambda k: acts[1 + a, k])
        masked_store((gg_out, gu_out)[a], (gmask, umask)[a], total, 2 * i, False)

    def grad_down(i):
        cols = pl.ds(256 * i, min(256, 896 - 256 * i))
        total = over_tokens(lambda k: acts[0, k, :, cols], lambda k: rows[1, k])
        masked_store(gd_out, dmask, total, 2 * i, True)

    steps = dict(
        G=gather_start, N=gather_step, E=gather_end, M=mask_weight, P=partial,
        F=rs_first, S=rs_second, L=rs_last, H=hidden, Q=act_grads,
        A=av_first, B=av_second, C=av_last, T=feature_part, Z=zr_step, Y=zr_last,
        W=grad_weight, D=grad_down,
    )
    for code, *indices in SCHEDULE:
        steps[code](*indices)
    for copy in sends:
        copy.wait_send()


def store_kernel(*refs):
    sems = refs[-1]
    copies = [pltpu.make_async_copy(refs[i], refs[5 + i], sems.at[i]) for i in range(5)]
    for copy in copies:
        copy.start()
    for copy in copies:
        copy.wait()


def shards(tokens, grad_output, gate_weight, up_weight, down_weight, gate_mask, up_mask, down_mask):
    anywhere = pl.BlockSpec(memory_space=pl.ANY)
    vmem = pl.BlockSpec(memory_space=pltpu.VMEM)
    dma = pltpu.SemaphoreType.DMA
    d1, d2 = PHASE_DTYPES
    n = CHUNKS
    pieces = 512 // PIECE
    shapes = [(64, 512), (64, 512), (512, 896), (512, 896), (896, 512)]
    results = pl.pallas_call(
        kernel,
        out_shape=[pltpu.VMEM(shape, BF) for shape in shapes],
        in_specs=[anywhere] * 8,
        out_specs=[vmem] * 5,
        scratch_shapes=[
            pltpu.VMEM((2, n, MANY, 512), BF),
            pltpu.VMEM((2, 512, 896), BF),
            pltpu.VMEM((896, 512), BF),
            pltpu.VMEM((3, n, MANY, 896), F32),
            pltpu.VMEM((3, n, 2, 6, MANY // 16, 896), d1),
            pltpu.VMEM((3, n, 2, 6, MANY // 16, 896), d1),
            pltpu.VMEM((3, n, 2, MANY // 8, 896), F32),
            pltpu.VMEM((3, n, 2, 6, MANY // 64, 896), d2),
            pltpu.VMEM((3, n, 2, 6, MANY // 64, 896), d2),
            pltpu.VMEM((3, n, 2, MANY // 32, 896), F32),
            pltpu.VMEM((3, n, MANY, 896), BF),
            pltpu.VMEM((2, n, pieces, 8, 2, OWN, PIECE), F32),
            pltpu.VMEM((2, n, pieces, 8, OWN, PIECE), F32),
            pltpu.VMEM((2, n, pieces, 2, 4, OWN, PIECE), F32),
            pltpu.VMEM((2, n, pieces, 2, 4, OWN, PIECE), F32),
            pltpu.SMEM((4, 7), jnp.int32),
            pltpu.SMEM((4, 7), jnp.int32),
            pltpu.SMEM((4, 7), jnp.int32),
            dma((2, n, 16)), dma((2, n, 16)),
            dma((3, n, 2, 12)), dma((3, n, 2, 12)),
            dma((3, n, 2, 8)), dma((3, n, 2, 8)),
            dma((2, n, pieces)), dma((2, n, pieces)),
            dma((2, n, pieces, 2, 4)), dma((2, n, pieces, 2, 4)),
            dma((2 * n + 6,)),
        ],
        compiler_params=pltpu.CompilerParams(
            collective_id=0, has_side_effects=True, vmem_limit_bytes=58_000_000
        ),
        name="ffn",
    )(
        tokens, grad_output, gate_weight, up_weight, down_weight, gate_mask, up_mask, down_mask.T
    )
    return tuple(
        pl.pallas_call(
            store_kernel,
            out_shape=[jax.ShapeDtypeStruct(shape, BF) for shape in shapes],
            in_specs=[anywhere] * 5,
            out_specs=[anywhere] * 5,
            scratch_shapes=[dma((5,))],
            name="store",
        )(*[pltpu.with_memory_space_constraint(result, pltpu.VMEM) for result in results])
    )


def solution(mesh):
    return jax.shard_map(
        shards,
        mesh=mesh,
        in_specs=(
            P("tensor", "dp"),
            P("tensor", "dp"),
            P("dp", "tensor"),
            P("dp", "tensor"),
            P("tensor", "dp"),
            P("dp", "tensor"),
            P("dp", "tensor"),
            P("tensor", "dp"),
        ),
        out_specs=(
            P("tensor", "dp"),
            P("tensor", "dp"),
            P("dp", "tensor"),
            P("dp", "tensor"),
            P("tensor", "dp"),
        ),
        check_vma=False,
    )
```

```python
import jax
import jax.numpy as jnp
from jax import lax
from jax.experimental import pallas as pl
from jax.experimental.pallas import tpu as pltpu
from jax.sharding import PartitionSpec as P

BF = jnp.bfloat16
F32 = jnp.float32
SIDE = 128
RING = 4
DEPTH = 8
CHUNKS = 2
OWN = 64 // CHUNKS
MANY = 1024 // CHUNKS
PIECE = 256
PHASE_DTYPES = (BF, F32)

SLOTS = (
    dict(FAR_R=0, FAR_L=1, OWN_R=2, OWN_L=3, SUM_R=4, SUM_L=5),
    dict(FAR_R=0, OWN_R=1, FAR_L=2, OWN_L=3, SUM_R=4, SUM_L=5),
)
SUMS = (pl.ds(0, 2), pl.ds(2, 1))
ACTS = (pl.ds(0, 1), pl.ds(1, 2))

SCHEDULE = (
    ("G", 0, 0),
    ("G", 1, 0),
    ("M", 0),
    ("M", 1),
    ("M", 2),
    ("N", 0, 0, 1),
    ("N", 0, 0, 7),
    ("N", 0, 0, 2),
    ("N", 0, 0, 6),
    ("N", 1, 0, 1),
    ("N", 1, 0, 2),
    ("N", 1, 0, 6),
    ("N", 1, 0, 7),
    ("G", 0, 1),
    ("N", 0, 0, 3),
    ("N", 0, 0, 5),
    ("N", 0, 0, 4),
    ("E", 0, 0),
    ("P", 0, 0),
    ("P", 1, 0),
    ("N", 1, 0, 4),
    ("F", 0, 0, 0, 0),
    ("F", 0, 0, 1, 0),
    ("N", 0, 1, 1),
    ("N", 0, 1, 2),
    ("N", 0, 1, 6),
    ("N", 0, 1, 7),
    ("G", 1, 1),
    ("N", 1, 0, 3),
    ("N", 1, 0, 5),
    ("E", 1, 0),
    ("P", 2, 0),
    ("F", 1, 0, 0, 0),
    ("F", 1, 0, 1, 0),
    ("S", 0, 0, 0, 0),
    ("S", 0, 0, 1, 0),
    ("N", 0, 1, 3),
    ("N", 0, 1, 4),
    ("N", 0, 1, 5),
    ("N", 1, 1, 1),
    ("N", 1, 1, 2),
    ("N", 1, 1, 7),
    ("N", 1, 1, 6),
    ("E", 0, 1),
    ("P", 0, 1),
    ("P", 1, 1),
    ("F", 0, 1, 0, 0),
    ("F", 0, 1, 1, 0),
    ("S", 1, 0, 0, 0),
    ("S", 1, 0, 1, 0),
    ("L", 0, 0, 0, 0),
    ("F", 0, 0, 0, 1),
    ("L", 0, 0, 1, 0),
    ("F", 0, 0, 1, 1),
    ("N", 1, 1, 3),
    ("N", 1, 1, 5),
    ("N", 1, 1, 4),
    ("S", 0, 1, 0, 0),
    ("E", 1, 1),
    ("P", 2, 1),
    ("F", 1, 1, 0, 0),
    ("F", 1, 1, 1, 0),
    ("S", 0, 1, 1, 0),
    ("L", 1, 0, 0, 0),
    ("F", 1, 0, 0, 1),
    ("L", 1, 0, 1, 0),
    ("F", 1, 0, 1, 1),
    ("S", 0, 0, 1, 1),
    ("S", 0, 0, 0, 1),
    ("S", 1, 1, 1, 0),
    ("L", 0, 1, 0, 0),
    ("F", 0, 1, 0, 1),
    ("S", 1, 1, 0, 0),
    ("L", 0, 1, 1, 0),
    ("F", 0, 1, 1, 1),
    ("S", 1, 0, 1, 1),
    ("S", 1, 0, 0, 1),
    ("L", 0, 0, 1, 1),
    ("H", 0, 1),
    ("L", 0, 0, 0, 1),
    ("H", 0, 0),
    ("L", 1, 1, 0, 0),
    ("F", 1, 1, 0, 1),
    ("L", 1, 1, 1, 0),
    ("F", 1, 1, 1, 1),
    ("S", 0, 1, 0, 1),
    ("S", 0, 1, 1, 1),
    ("L", 1, 0, 0, 1),
    ("Q", 0, 0),
    ("L", 1, 0, 1, 1),
    ("Q", 0, 1),
    ("B", 0, 0, 0, 0),
    ("B", 0, 0, 1, 0),
    ("S", 1, 1, 0, 1),
    ("S", 1, 1, 1, 1),
    ("L", 0, 1, 0, 1),
    ("H", 1, 0),
    ("L", 0, 1, 1, 1),
    ("H", 1, 1),
    ("B", 1, 0, 0, 0),
    ("B", 1, 0, 1, 0),
    ("C", 0, 0, 0, 0),
    ("A", 0, 0, 0, 1),
    ("C", 0, 0, 1, 0),
    ("A", 0, 0, 1, 1),
    ("L", 1, 1, 0, 1),
    ("Q", 1, 0),
    ("L", 1, 1, 1, 1),
    ("Q", 1, 1),
    ("B", 0, 1, 0, 0),
    ("B", 0, 1, 1, 0),
    ("C", 1, 0, 0, 0),
    ("A", 1, 0, 0, 1),
    ("C", 1, 0, 1, 0),
    ("A", 1, 0, 1, 1),
    ("B", 0, 0, 1, 1),
    ("B", 0, 0, 0, 1),
    ("B", 1, 1, 0, 0),
    ("B", 1, 1, 1, 0),
    ("C", 0, 1, 0, 0),
    ("A", 0, 1, 0, 1),
    ("C", 0, 1, 1, 0),
    ("A", 0, 1, 1, 1),
    ("B", 1, 0, 1, 1),
    ("B", 1, 0, 0, 1),
    ("C", 0, 0, 1, 1),
    ("C", 0, 0, 0, 1),
    ("T", 0, 0, 0, 0),
    ("T", 0, 0, 0, 1),
    ("C", 1, 1, 0, 0),
    ("C", 1, 1, 1, 0),
    ("A", 1, 1, 0, 1),
    ("A", 1, 1, 1, 1),
    ("Z", 0, 0, 0, 4),
    ("B", 0, 1, 0, 1),
    ("B", 0, 1, 1, 1),
    ("Z", 0, 0, 1, 4),
    ("C", 1, 0, 0, 1),
    ("C", 1, 0, 1, 1),
    ("T", 1, 1, 0, 0),
    ("T", 1, 1, 0, 1),
    ("T", 1, 2, 0, 0),
    ("T", 1, 2, 0, 1),
    ("Z", 0, 0, 0, 3),
    ("Z", 0, 0, 1, 3),
    ("Z", 1, 0, 0, 4),
    ("Z", 1, 0, 1, 4),
    ("B", 1, 1, 0, 1),
    ("B", 1, 1, 1, 1),
    ("Z", 0, 0, 0, 2),
    ("C", 0, 1, 0, 1),
    ("C", 0, 1, 1, 1),
    ("D", 2),
    ("Z", 0, 0, 1, 2),
    ("T", 0, 0, 1, 1),
    ("Z", 1, 0, 0, 3),
    ("D", 0),
    ("D", 1),
    ("Z", 1, 0, 1, 3),
    ("D", 3),
    ("T", 0, 0, 1, 0),
    ("Z", 0, 1, 1, 4),
    ("Z", 0, 0, 0, 1),
    ("C", 1, 1, 0, 1),
    ("Z", 0, 0, 1, 1),
    ("C", 1, 1, 1, 1),
    ("T", 1, 1, 1, 0),
    ("T", 1, 2, 1, 0),
    ("Z", 0, 1, 0, 4),
    ("Z", 1, 0, 0, 2),
    ("T", 1, 1, 1, 1),
    ("T", 1, 2, 1, 1),
    ("Z", 1, 0, 1, 2),
    ("W", 0, 0),
    ("Z", 0, 1, 1, 3),
    ("W", 1, 0),
    ("Y", 0, 0, 0),
    ("Z", 1, 1, 0, 4),
    ("W", 1, 1),
    ("W", 0, 1),
    ("Y", 0, 0, 1),
    ("Z", 1, 1, 1, 4),
    ("Z", 0, 1, 0, 3),
    ("Z", 1, 0, 0, 1),
    ("Z", 1, 0, 1, 1),
    ("Z", 0, 1, 1, 2),
    ("Z", 1, 1, 0, 3),
    ("Z", 1, 1, 1, 3),
    ("Z", 0, 1, 0, 2),
    ("Y", 1, 0, 0),
    ("Y", 1, 0, 1),
    ("Z", 0, 1, 1, 1),
    ("Z", 1, 1, 0, 2),
    ("Z", 1, 1, 1, 2),
    ("Z", 0, 1, 0, 1),
    ("Y", 0, 1, 1),
    ("Z", 1, 1, 0, 1),
    ("Z", 1, 1, 1, 1),
    ("Y", 0, 1, 0),
    ("Y", 1, 1, 0),
    ("Y", 1, 1, 1),
)


def mm(left, right_side, dims):
    return lax.dot_general(left, right_side, (dims, ((), ())), preferred_element_type=F32)


def kernel(
    tok_in, cot_in, wg_in, wu_in, wd_in, gm_in, um_in, dm_in,
    o_out, gt_out, gg_out, gu_out, gd_out,
    rows, weights, weight_d, part, sent1, got1, acc1, sent2, got2, fin,
    acts, outs, peer, zsent, zgot, gmask, umask, dmask,
    z_s, ag_r, rs_s, rs_r, av_s, av_r, ex_s, ex_r, zr_s, zr_r, loc,
):
    dp = lax.axis_index("dp")
    tensor = lax.axis_index("tensor")
    x, y = dp // RING, dp % RING
    z, core = tensor // 2, tensor % 2

    def wrap(value, n):
        return lax.rem(value + 2 * n, n)

    def at(dx=0, dy=0, dz=0, dc=0):
        return {
            "dp": wrap(x + dx, RING) * RING + wrap(y + dy, RING),
            "tensor": wrap(z + dz, DEPTH) * 2 + (1 - core if dc else core),
        }

    def remote(src, dst, s_sem, r_sem, device):
        return pltpu.make_async_remote_copy(
            src_ref=src, dst_ref=dst, send_sem=s_sem, recv_sem=r_sem,
            device_id=device, device_id_type=pl.DeviceIdType.MESH,
        )

    def push(src, dst, s_sem, r_sem, device):
        remote(src, dst, s_sem, r_sem, device).start()

    def arrived(dst, s_sem, r_sem):
        remote(dst, dst, s_sem, r_sem, at(dz=1)).wait_recv()

    def sent_all(src, s_sem):
        remote(src, src, s_sem, ex_r.at[0, 0, 0], at(dz=1)).wait_send()

    def block(i, k, zz, cc):
        return rows.at[i, k, wrap(zz, DEPTH), cc]

    row_loads = [
        [
            pltpu.make_async_copy(
                ref.at[pl.ds(OWN * k, OWN)], block(i, k, z, core), loc.at[CHUNKS * i + k]
            )
            for k in range(CHUNKS)
        ]
        for i, ref in enumerate((tok_in, cot_in))
    ]
    other_loads = [
        pltpu.make_async_copy(src, dst, loc.at[2 * CHUNKS + n])
        for n, (src, dst) in enumerate(
            (
                (gm_in, gmask), (um_in, umask), (dm_in, dmask),
                (wg_in, weights.at[0]), (wu_in, weights.at[1]), (wd_in, weight_d),
            )
        )
    ]
    for load in row_loads[0] + row_loads[1] + other_loads:
        load.start()

    barrier = pltpu.get_barrier_semaphore()
    peers = [at(dx=1), at(dx=-1), at(dy=1), at(dy=-1), at(dc=1)]
    peers += [at(dz=d) for d in (1, -1, 2, -2)]
    for device in peers:
        pl.semaphore_signal(barrier, inc=1, device_id=device, device_id_type=pl.DeviceIdType.MESH)
    pl.semaphore_wait(barrier, len(peers))

    up, down, other = at(dz=1), at(dz=-1), at(dc=1)

    def z_push(i, k, slot, ref, device):
        push(ref, ref, z_s.at[0], ag_r.at[i, k, slot], device)

    def z_share(i, k, zz):
        ref = block(i, k, zz, core)
        push(ref, ref, z_s.at[1], ag_r.at[i, k, 0], other)

    def z_arrived(i, k, slot, ref):
        arrived(ref, z_s.at[0], ag_r.at[i, k, slot])

    def gather_start(i, k):
        row_loads[i][k].wait()
        z_share(i, k, z)
        for d in (2, -2, 1, -1):
            z_push(i, k, d % DEPTH, block(i, k, z, core), at(dz=d))

    def gather_step(i, k, d):
        n = d if d < 4 else d - DEPTH
        ref = block(i, k, z - n, core)
        z_arrived(i, k, d, ref)
        if abs(n) == 1:
            z_push(i, k, 3 * n % DEPTH, ref, at(dz=2 * n))
        elif abs(n) == 2:
            z_push(i, k, 4, ref.at[pl.ds(0 if n > 0 else OWN // 2, OWN // 2)], at(dz=n))
        z_share(i, k, z - n)

    def gather_end(i, k):
        arrived(rows.at[i, k, :, 1 - core], z_s.at[1], ag_r.at[i, k, 0])

    def keep(mask, i, j):
        return mask[i, j].astype(F32)

    def mask_weight(n):
        for load in (other_loads[n], other_loads[3 + n]):
            load.wait()
        ref = weight_d if n == 2 else weights.at[n]
        n_rows, n_cols = (7, 4) if n == 2 else (4, 7)

        def body(i, carry):
            rows_i = pl.ds(pl.multiple_of(i * SIDE, SIDE), SIDE)
            for j in range(n_cols):
                cols = pl.ds(j * SIDE, SIDE)
                factor = keep(dmask, j, i) if n == 2 else keep((gmask, umask)[n], i, j)
                ref[rows_i, cols] = (ref[rows_i, cols].astype(F32) * factor).astype(BF)
            return carry

        lax.fori_loop(0, n_rows, body, 0)

    def tiles(body):
        def step(i, carry):
            body(i, pl.ds(pl.multiple_of(i * 256, 256), 256))
            return carry

        lax.fori_loop(0, MANY // 256, step, 0)

    def tile_rows(j, k, i):
        n = 256 // (2 * OWN)
        return rows[j, k, pl.ds(n * i, n)].reshape(256, 512)

    def partial(a, k):
        def body(i, where):
            if a < 2:
                part[a, k, where] = mm(tile_rows(0, k, i), weights[a], ((1,), (0,)))
            else:
                part[2, k, where] = mm(tile_rows(1, k, i), weight_d[...], ((1,), (1,)))

        tiles(body)

    def ring(h, phase):
        if (h + phase) % 2 == 0:
            return x, at(dx=1), at(dx=-1)
        return y, at(dy=1), at(dy=-1)

    def rs_refs(u, k, h, phase):
        which = SUMS[u]
        if phase == 0:
            return (
                part.at[which, k], h * (MANY // 2), MANY // 16,
                sent1.at[which, k, h], got1.at[which, k, h], acc1.at[which, k, h],
            )
        return (
            acc1.at[which, k, h], 0, MANY // 64,
            sent2.at[which, k, h], got2.at[which, k, h], fin.at[which, k, h],
        )

    def rs_sems(u, k, h, phase, n):
        return rs_s.at[phase], rs_r.at[u, k, h, 3 * phase + n]

    def rs_push(u, k, h, phase, first, count, n, device):
        _, _, _, sent, got, _ = rs_refs(u, k, h, phase)
        where = pl.ds(first, count)
        push(sent.at[:, where], got.at[:, where], *rs_sems(u, k, h, phase, n), device)

    def rs_arrived(u, k, h, phase, first, count, n):
        got = rs_refs(u, k, h, phase)[4]
        arrived(got.at[:, pl.ds(first, count)], *rs_sems(u, k, h, phase, n))

    def rs_block(u, k, h, phase, d, second):
        src, base, n, _, _, _ = rs_refs(u, k, h, phase)
        start = base + 2 * n * d + n * second
        return src[:, pl.ds(pl.multiple_of(start, n), n), :]

    def rs_first(u, k, h, phase):
        q, right, left = ring(h, phase)
        sent = rs_refs(u, k, h, phase)[3]
        dtype = PHASE_DTYPES[phase]
        slots = SLOTS[phase]
        far, to_r, to_l = wrap(q + 2, RING), wrap(q + 1, RING), wrap(q - 1, RING)
        plan = (
            ("FAR_R", far, 0, right, 0), ("FAR_L", far, 1, left, 1),
            ("OWN_R", to_r, 1, right, 2), ("OWN_L", to_l, 0, left, 2),
        )
        for name, d, second, device, n in plan:
            sent[:, slots[name]] = rs_block(u, k, h, phase, d, second).astype(dtype)
            if phase == 0:
                rs_push(u, k, h, 0, slots[name], 1, n, device)
            elif n == 2:
                rs_push(u, k, h, 1, slots[name] - 1, 2, 0 if device is right else 1, device)

    def rs_second(u, k, h, phase):
        q, right, left = ring(h, phase)
        _, _, _, sent, got, _ = rs_refs(u, k, h, phase)
        dtype = PHASE_DTYPES[phase]
        slots = SLOTS[phase]
        for way, d, second, device, n in (
            ("_R", wrap(q + 1, RING), 0, right, 0), ("_L", wrap(q - 1, RING), 1, left, 1),
        ):
            far, out = slots["FAR" + way], slots["SUM" + way]
            rs_arrived(u, k, h, phase, far, 1 + phase, n)
            sent[:, out] = (rs_block(u, k, h, phase, d, second) + got[:, far].astype(F32)).astype(dtype)
            rs_push(u, k, h, phase, out, 1, 2, device)

    def rs_last(u, k, h, phase):
        q = ring(h, phase)[0]
        _, _, n, _, got, dst = rs_refs(u, k, h, phase)
        slots = SLOTS[phase]
        rs_arrived(u, k, h, phase, 2 + 2 * phase, 4 - 2 * phase, 2)
        for second, one, two in ((0, "SUM_R", "OWN_L"), (1, "OWN_R", "SUM_L")):
            dst[:, pl.ds(n * second, n), :] = (
                rs_block(u, k, h, phase, q, second)
                + got[:, slots[one]].astype(F32) + got[:, slots[two]].astype(F32)
            )

    def av_rows(h, phase, d, second=None):
        n = MANY // 32 if phase == 0 else MANY // 8
        start = h * (MANY // 2) + n * d
        if phase == 0:
            start = start + MANY // 8 * ring(h, 0)[0]
        if second is None:
            return pl.ds(pl.multiple_of(start, n), n)
        return pl.ds(pl.multiple_of(start + n // 2 * second, n // 2), n // 2)

    def av_move(v, k, h, phase, slot, where, device=None):
        ref = acts.at[ACTS[v], k, where]
        sems = av_s.at[0], av_r.at[v, k, h, 3 * phase + slot]
        if device is None:
            arrived(ref, *sems)
        else:
            push(ref, ref, *sems, device)

    def av_first(v, k, h, phase):
        q, right, left = ring(h, 1 - phase)
        av_move(v, k, h, phase, 0, av_rows(h, phase, q), right)
        av_move(v, k, h, phase, 1, av_rows(h, phase, q), left)

    def av_second(v, k, h, phase):
        q, right, left = ring(h, 1 - phase)
        for slot, d, device, part_of in (
            (0, wrap(q - 1, RING), right, 0), (1, wrap(q + 1, RING), left, 1),
        ):
            av_move(v, k, h, phase, slot, av_rows(h, phase, d))
            if phase == 1:
                av_move(v, k, h, 1, 2, av_rows(h, 1, d, part_of), device)
            elif (v + k + h) % 2 == slot:
                av_move(v, k, h, 0, 2, av_rows(h, 0, d), device)

    def av_last(v, k, h, phase):
        q = ring(h, 1 - phase)[0]
        av_move(v, k, h, phase, 2, av_rows(h, phase, wrap(q + 2, RING)))

    def own_rows(h):
        return av_rows(h, 0, ring(h, 1)[0])

    def hidden(k, h):
        gate = fin[0, k, h]
        acts[0, k, own_rows(h)] = (gate * jax.nn.sigmoid(gate) * fin[1, k, h]).astype(BF)
        av_first(0, k, h, 0)

    def act_grads(k, h):
        gate, upv, grad = fin[0, k, h], fin[1, k, h], fin[2, k, h]
        s = jax.nn.sigmoid(gate)
        acts[1, k, own_rows(h)] = (grad * upv * s * (1.0 + gate * (1.0 - s))).astype(BF)
        acts[2, k, own_rows(h)] = (grad * (gate * s)).astype(BF)
        av_first(1, k, h, 0)

    def feature_part(b, a, k, c):
        cols = pl.ds(c * PIECE, PIECE)
        n = 256 // (2 * OWN)

        def body(i, where):
            if a == 0:
                tile = mm(acts[0, k, where], weight_d[:, cols], ((1,), (0,)))
            else:
                tile = mm(acts[a, k, where], weights[a - 1, cols, :], ((1,), (1,)))
            tile = tile.reshape(n, 2, OWN, PIECE)
            if a == 2:
                tile = tile + outs[b, k, c, pl.ds(n * i, n)]
            outs[b, k, c, pl.ds(n * i, n)] = tile

        tiles(body)
        if a != 1:
            push(outs.at[b, k, c, :, 1 - core], peer.at[b, k, c], ex_s.at[0], ex_r.at[b, k, c], other)

    def zr_move(b, k, c, way, n, send):
        where = pl.ds(0, OWN) if n < 4 else pl.ds(OWN // 2 * way, OWN // 2)
        sems = zr_s.at[n // 4], zr_r.at[b, k, c, 3 * way + n - 2 if n > 1 else 6]
        got = zgot.at[b, k, c, way, n - 1, where]
        if send:
            push(zsent.at[b, k, c, way, n - 1, where], got, *sems, (up, down)[way])
        else:
            arrived(got, *sems)

    def zr_step(b, k, c, n):
        if n == 4:
            arrived(peer.at[b, k, c], ex_s.at[0], ex_r.at[b, k, c])
        for way in range(2):
            target = wrap(z + n if way == 0 else z - n, DEPTH)
            if n == 4:
                where = pl.ds(OWN // 2 * way, OWN // 2)
                zsent[b, k, c, way, 3, where] = (
                    outs[b, k, c, target, core, where] + peer[b, k, c, target, where]
                )
            else:
                zr_move(b, k, c, way, n + 1, False)
                if n == 3:
                    fresh, rest = pl.ds(OWN // 2 * way, OWN // 2), pl.ds(OWN // 2 * (1 - way), OWN // 2)
                    zsent[b, k, c, way, 2, rest] = (
                        outs[b, k, c, target, core, rest] + peer[b, k, c, target, rest]
                    )
                    zsent[b, k, c, way, 2, fresh] = (
                        outs[b, k, c, target, core, fresh] + peer[b, k, c, target, fresh]
                        + zgot[b, k, c, way, 3, fresh]
                    )
                else:
                    zsent[b, k, c, way, n - 1] = (
                        outs[b, k, c, target, core] + peer[b, k, c, target] + zgot[b, k, c, way, n]
                    )
            zr_move(b, k, c, way, n, True)

    def zr_last(b, k, c):
        arrived(zgot.at[b, k, c, :, 0], zr_s.at[0], zr_r.at[b, k, c, 6])
        total = outs[b, k, c, z, core] + peer[b, k, c, z] + zgot[b, k, c, 0, 0] + zgot[b, k, c, 1, 0]
        (o_out, gt_out)[b][pl.ds(OWN * k, OWN), pl.ds(c * PIECE, PIECE)] = total.astype(BF)

    def over_tokens(left, right_side):
        total = mm(left(0).T, right_side(0), ((1,), (0,)))
        for k in range(1, CHUNKS):
            total = total + mm(left(k).T, right_side(k), ((1,), (0,)))
        return total

    def masked_store(out, mask, total, row, flip):
        for r in range(total.shape[0] // SIDE):
            for j in range(total.shape[1] // SIDE):
                factor = keep(mask, j, row + r) if flip else keep(mask, row + r, j)
                out[pl.ds((row + r) * SIDE, SIDE), pl.ds(j * SIDE, SIDE)] = (
                    total[r * SIDE : (r + 1) * SIDE, j * SIDE : (j + 1) * SIDE] * factor
                ).astype(BF)

    def grad_weight(a, i):
        cols = pl.ds(256 * i, 256)
        total = over_tokens(lambda k: rows[0, k, :, :, :, cols].reshape(MANY, 256), lambda k: acts[1 + a, k])
        masked_store((gg_out, gu_out)[a], (gmask, umask)[a], total, 2 * i, False)

    def grad_down(i):
        cols = pl.ds(256 * i, min(256, 896 - 256 * i))
        total = over_tokens(lambda k: acts[0, k, :, cols], lambda k: rows[1, k].reshape(MANY, 512))
        masked_store(gd_out, dmask, total, 2 * i, True)

    steps = dict(
        G=gather_start, N=gather_step, E=gather_end, M=mask_weight, P=partial,
        F=rs_first, S=rs_second, L=rs_last, H=hidden, Q=act_grads,
        A=av_first, B=av_second, C=av_last, T=feature_part, Z=zr_step, Y=zr_last,
        W=grad_weight, D=grad_down,
    )
    for code, *indices in SCHEDULE:
        steps[code](*indices)
    sent_all(rows.at[:, :, pl.ds(0, DEPTH - 1), 0], z_s.at[0])
    sent_all(rows.at[:, :, :, 0], z_s.at[1])
    sent_all(sent1, rs_s.at[0])
    sent_all(sent2, rs_s.at[1])
    sent_all(acts.at[:, :, pl.ds(0, MANY // 16 * 15)], av_s.at[0])
    sent_all(peer, ex_s.at[0])
    sent_all(zsent.at[:, :, :, :, pl.ds(0, 3)], zr_s.at[0])
    sent_all(zsent.at[:, :, :, :, 3, pl.ds(0, OWN // 2)], zr_s.at[1])


def store_kernel(*refs):
    sems = refs[-1]
    copies = [pltpu.make_async_copy(refs[i], refs[5 + i], sems.at[i]) for i in range(5)]
    for copy in copies:
        copy.start()
    for copy in copies:
        copy.wait()


def shards(tokens, grad_output, gate_weight, up_weight, down_weight, gate_mask, up_mask, down_mask):
    anywhere = pl.BlockSpec(memory_space=pl.ANY)
    vmem = pl.BlockSpec(memory_space=pltpu.VMEM)
    dma = pltpu.SemaphoreType.DMA
    d1, d2 = PHASE_DTYPES
    n = CHUNKS
    pieces = 512 // PIECE
    shapes = [(64, 512), (64, 512), (512, 896), (512, 896), (896, 512)]
    results = pl.pallas_call(
        kernel,
        out_shape=[pltpu.VMEM(shape, BF) for shape in shapes],
        in_specs=[anywhere] * 8,
        out_specs=[vmem] * 5,
        scratch_shapes=[
            pltpu.VMEM((2, n, DEPTH, 2, OWN, 512), BF),
            pltpu.VMEM((2, 512, 896), BF),
            pltpu.VMEM((896, 512), BF),
            pltpu.VMEM((3, n, MANY, 896), F32),
            pltpu.VMEM((3, n, 2, 6, MANY // 16, 896), d1),
            pltpu.VMEM((3, n, 2, 6, MANY // 16, 896), d1),
            pltpu.VMEM((3, n, 2, MANY // 8, 896), F32),
            pltpu.VMEM((3, n, 2, 6, MANY // 64, 896), d2),
            pltpu.VMEM((3, n, 2, 6, MANY // 64, 896), d2),
            pltpu.VMEM((3, n, 2, MANY // 32, 896), F32),
            pltpu.VMEM((3, n, MANY, 896), BF),
            pltpu.VMEM((2, n, pieces, 8, 2, OWN, PIECE), F32),
            pltpu.VMEM((2, n, pieces, 8, OWN, PIECE), F32),
            pltpu.VMEM((2, n, pieces, 2, 4, OWN, PIECE), F32),
            pltpu.VMEM((2, n, pieces, 2, 4, OWN, PIECE), F32),
            pltpu.SMEM((4, 7), jnp.int32),
            pltpu.SMEM((4, 7), jnp.int32),
            pltpu.SMEM((4, 7), jnp.int32),
            dma((2,)), dma((2, n, 8)),
            dma((2,)), dma((2, n, 2, 6)),
            dma((1,)), dma((2, n, 2, 6)),
            dma((1,)), dma((2, n, pieces)),
            dma((2,)), dma((2, n, pieces, 7)),
            dma((2 * n + 6,)),
        ],
        compiler_params=pltpu.CompilerParams(
            collective_id=0, has_side_effects=True, vmem_limit_bytes=58_000_000
        ),
        name="ffn",
    )(
        tokens, grad_output, gate_weight, up_weight, down_weight, gate_mask, up_mask, down_mask.T
    )
    return tuple(
        pl.pallas_call(
            store_kernel,
            out_shape=[jax.ShapeDtypeStruct(shape, BF) for shape in shapes],
            in_specs=[anywhere] * 5,
            out_specs=[anywhere] * 5,
            scratch_shapes=[dma((5,))],
            name="store",
        )(*[pltpu.with_memory_space_constraint(result, pltpu.VMEM) for result in results])
    )


def solution(mesh):
    return jax.shard_map(
        shards,
        mesh=mesh,
        in_specs=(
            P("tensor", "dp"),
            P("tensor", "dp"),
            P("dp", "tensor"),
            P("dp", "tensor"),
            P("tensor", "dp"),
            P("dp", "tensor"),
            P("dp", "tensor"),
            P("tensor", "dp"),
        ),
        out_specs=(
            P("tensor", "dp"),
            P("tensor", "dp"),
            P("dp", "tensor"),
            P("dp", "tensor"),
            P("tensor", "dp"),
        ),
        check_vma=False,
    )
```

```python
import jax
import jax.numpy as jnp
from jax import lax
from jax.experimental import pallas as pl
from jax.experimental.pallas import tpu as pltpu
from jax.sharding import PartitionSpec as P

BF = jnp.bfloat16
F32 = jnp.float32
SIDE = 128
RING = 4
DEPTH = 8
CHUNKS = 2
OWN = 64 // CHUNKS
MANY = 1024 // CHUNKS
PIECE = 256
PHASE_DTYPES = (BF, F32)

SLOTS = (
    dict(FAR_R=0, FAR_L=1, OWN_R=2, OWN_L=3, SUM_R=4, SUM_L=5),
    dict(FAR_R=0, OWN_R=1, FAR_L=2, OWN_L=3, SUM_R=4, SUM_L=5),
)
SUMS = (pl.ds(0, 2), pl.ds(2, 1))
ACTS = (pl.ds(0, 1), pl.ds(1, 2))

SCHEDULE = (
    ("G", 0, 0),
    ("G", 1, 0),
    ("M", 0),
    ("M", 1),
    ("M", 2),
    ("N", 0, 0, 1),
    ("N", 0, 0, 7),
    ("N", 0, 0, 6),
    ("N", 0, 0, 2),
    ("N", 1, 0, 1),
    ("N", 1, 0, 2),
    ("N", 1, 0, 6),
    ("N", 1, 0, 7),
    ("G", 0, 1),
    ("N", 0, 0, 3),
    ("N", 0, 0, 5),
    ("N", 0, 0, 4),
    ("E", 0, 0),
    ("P", 1, 0),
    ("N", 1, 0, 3),
    ("P", 0, 0),
    ("N", 1, 0, 4),
    ("F", 0, 0, 0, 0),
    ("N", 1, 0, 5),
    ("F", 0, 0, 1, 0),
    ("N", 0, 1, 1),
    ("N", 0, 1, 2),
    ("N", 0, 1, 6),
    ("N", 0, 1, 7),
    ("G", 1, 1),
    ("E", 1, 0),
    ("P", 2, 0),
    ("F", 1, 0, 0, 0),
    ("F", 1, 0, 1, 0),
    ("S", 0, 0, 0, 0),
    ("S", 0, 0, 1, 0),
    ("N", 0, 1, 3),
    ("N", 0, 1, 4),
    ("N", 0, 1, 5),
    ("N", 1, 1, 1),
    ("N", 1, 1, 2),
    ("E", 0, 1),
    ("P", 1, 1),
    ("N", 1, 1, 6),
    ("N", 1, 1, 7),
    ("P", 0, 1),
    ("S", 1, 0, 0, 0),
    ("S", 1, 0, 1, 0),
    ("F", 0, 1, 0, 0),
    ("F", 0, 1, 1, 0),
    ("L", 0, 0, 0, 0),
    ("F", 0, 0, 0, 1),
    ("L", 0, 0, 1, 0),
    ("F", 0, 0, 1, 1),
    ("N", 1, 1, 3),
    ("L", 1, 0, 0, 0),
    ("N", 1, 1, 4),
    ("F", 1, 0, 0, 1),
    ("L", 1, 0, 1, 0),
    ("F", 1, 0, 1, 1),
    ("N", 1, 1, 5),
    ("E", 1, 1),
    ("P", 2, 1),
    ("F", 1, 1, 0, 0),
    ("S", 0, 1, 1, 0),
    ("S", 0, 1, 0, 0),
    ("F", 1, 1, 1, 0),
    ("S", 0, 0, 1, 1),
    ("S", 0, 0, 0, 1),
    ("S", 1, 0, 1, 1),
    ("S", 1, 0, 0, 1),
    ("S", 1, 1, 0, 0),
    ("L", 0, 1, 1, 0),
    ("F", 0, 1, 1, 1),
    ("S", 1, 1, 1, 0),
    ("L", 0, 1, 0, 0),
    ("F", 0, 1, 0, 1),
    ("L", 0, 0, 1, 1),
    ("H", 0, 1),
    ("L", 0, 0, 0, 1),
    ("H", 0, 0),
    ("L", 1, 0, 1, 1),
    ("Q", 0, 1),
    ("L", 1, 0, 0, 1),
    ("Q", 0, 0),
    ("L", 1, 1, 0, 0),
    ("F", 1, 1, 0, 1),
    ("L", 1, 1, 1, 0),
    ("F", 1, 1, 1, 1),
    ("S", 0, 1, 1, 1),
    ("B", 0, 0, 1, 0),
    ("S", 0, 1, 0, 1),
    ("B", 0, 0, 0, 0),
    ("B", 1, 0, 1, 0),
    ("B", 1, 0, 0, 0),
    ("S", 1, 1, 1, 1),
    ("S", 1, 1, 0, 1),
    ("L", 0, 1, 1, 1),
    ("H", 1, 1),
    ("C", 0, 0, 1, 0),
    ("A", 0, 0, 1, 1),
    ("L", 0, 1, 0, 1),
    ("H", 1, 0),
    ("C", 0, 0, 0, 0),
    ("A", 0, 0, 0, 1),
    ("C", 1, 0, 1, 0),
    ("A", 1, 0, 1, 1),
    ("L", 1, 1, 1, 1),
    ("Q", 1, 1),
    ("C", 1, 0, 0, 0),
    ("A", 1, 0, 0, 1),
    ("L", 1, 1, 0, 1),
    ("Q", 1, 0),
    ("B", 0, 1, 1, 0),
    ("B", 0, 0, 1, 1),
    ("B", 0, 0, 0, 1),
    ("B", 0, 1, 0, 0),
    ("B", 1, 1, 1, 0),
    ("B", 1, 0, 1, 1),
    ("B", 1, 0, 0, 1),
    ("B", 1, 1, 0, 0),
    ("C", 0, 1, 1, 0),
    ("A", 0, 1, 1, 1),
    ("C", 0, 0, 1, 1),
    ("C", 0, 1, 0, 0),
    ("A", 0, 1, 0, 1),
    ("C", 0, 0, 0, 1),
    ("T", 0, 0, 0, 0),
    ("T", 0, 0, 0, 1),
    ("C", 1, 1, 1, 0),
    ("A", 1, 1, 1, 1),
    ("C", 1, 0, 1, 1),
    ("Z", 0, 0, 0, 4),
    ("C", 1, 1, 0, 0),
    ("A", 1, 1, 0, 1),
    ("C", 1, 0, 0, 1),
    ("T", 1, 1, 0, 0),
    ("T", 1, 1, 0, 1),
    ("T", 1, 2, 0, 0),
    ("B", 0, 1, 1, 1),
    ("T", 1, 2, 0, 1),
    ("B", 0, 1, 0, 1),
    ("Z", 0, 0, 1, 4),
    ("Z", 1, 0, 0, 4),
    ("Z", 0, 0, 0, 3),
    ("Z", 1, 0, 1, 4),
    ("B", 1, 1, 1, 1),
    ("Z", 0, 0, 1, 3),
    ("B", 1, 1, 0, 1),
    ("Z", 1, 0, 0, 3),
    ("Z", 0, 0, 0, 2),
    ("Z", 1, 0, 1, 3),
    ("C", 0, 1, 1, 1),
    ("C", 0, 1, 0, 1),
    ("T", 0, 0, 1, 0),
    ("T", 0, 0, 1, 1),
    ("Z", 0, 0, 1, 2),
    ("D", 0),
    ("D", 1),
    ("C", 1, 1, 1, 1),
    ("Z", 1, 0, 0, 2),
    ("D", 2),
    ("Z", 0, 0, 0, 1),
    ("C", 1, 1, 0, 1),
    ("T", 1, 1, 1, 0),
    ("T", 1, 1, 1, 1),
    ("T", 1, 2, 1, 0),
    ("Z", 0, 1, 0, 4),
    ("Z", 0, 1, 1, 4),
    ("Z", 1, 0, 1, 2),
    ("T", 1, 2, 1, 1),
    ("D", 3),
    ("Z", 0, 0, 1, 1),
    ("W", 0, 0),
    ("Z", 1, 1, 0, 4),
    ("W", 0, 1),
    ("Z", 1, 0, 0, 1),
    ("W", 1, 0),
    ("Z", 1, 1, 1, 4),
    ("Y", 0, 0, 0),
    ("W", 1, 1),
    ("Z", 0, 1, 0, 3),
    ("Z", 0, 1, 1, 3),
    ("Z", 1, 0, 1, 1),
    ("Y", 0, 0, 1),
    ("Z", 1, 1, 0, 3),
    ("Y", 1, 0, 0),
    ("Z", 1, 1, 1, 3),
    ("Z", 0, 1, 0, 2),
    ("Z", 0, 1, 1, 2),
    ("Y", 1, 0, 1),
    ("Z", 1, 1, 0, 2),
    ("Z", 1, 1, 1, 2),
    ("Z", 0, 1, 0, 1),
    ("Z", 0, 1, 1, 1),
    ("Z", 1, 1, 0, 1),
    ("Z", 1, 1, 1, 1),
    ("Y", 0, 1, 0),
    ("Y", 0, 1, 1),
    ("Y", 1, 1, 0),
    ("Y", 1, 1, 1),
)


def mm(left, right_side, dims):
    return lax.dot_general(left, right_side, (dims, ((), ())), preferred_element_type=F32)


def kernel(
    tok_in, cot_in, wg_in, wu_in, wd_in, gm_in, um_in, dm_in,
    o_out, gt_out, gg_out, gu_out, gd_out,
    rows, weights, weight_d, part, sent1, got1, acc1, sent2, got2, fin,
    acts, outs, peer, zsent, zgot, gmask, umask, dmask,
    z_s, ag_r, rs_s, rs_r, av_s, av_r, ex_s, ex_r, zr_s, zr_r, loc,
):
    dp = lax.axis_index("dp")
    tensor = lax.axis_index("tensor")
    x, y = dp // RING, dp % RING
    z, core = tensor // 2, tensor % 2

    def wrap(value, n):
        return lax.rem(value + 2 * n, n)

    def at(dx=0, dy=0, dz=0, dc=0):
        return {
            "dp": wrap(x + dx, RING) * RING + wrap(y + dy, RING),
            "tensor": wrap(z + dz, DEPTH) * 2 + (1 - core if dc else core),
        }

    def remote(src, dst, s_sem, r_sem, device):
        return pltpu.make_async_remote_copy(
            src_ref=src, dst_ref=dst, send_sem=s_sem, recv_sem=r_sem,
            device_id=device, device_id_type=pl.DeviceIdType.MESH,
        )

    def push(src, dst, s_sem, r_sem, device):
        remote(src, dst, s_sem, r_sem, device).start()

    def arrived(dst, s_sem, r_sem):
        remote(dst, dst, s_sem, r_sem, at(dz=1)).wait_recv()

    def sent_all(src, s_sem):
        remote(src, src, s_sem, ex_r.at[0, 0, 0], at(dz=1)).wait_send()

    def block(i, k, zz, cc):
        return rows.at[i, k, wrap(zz, DEPTH), cc]

    row_loads = [
        [
            pltpu.make_async_copy(
                ref.at[pl.ds(OWN * k, OWN)], block(i, k, z, core), loc.at[CHUNKS * i + k]
            )
            for k in range(CHUNKS)
        ]
        for i, ref in enumerate((tok_in, cot_in))
    ]
    other_loads = [
        pltpu.make_async_copy(src, dst, loc.at[2 * CHUNKS + n])
        for n, (src, dst) in enumerate(
            (
                (gm_in, gmask), (um_in, umask), (dm_in, dmask),
                (wg_in, weights.at[0]), (wu_in, weights.at[1]), (wd_in, weight_d),
            )
        )
    ]
    for load in row_loads[0] + row_loads[1] + other_loads:
        load.start()

    barrier = pltpu.get_barrier_semaphore()
    peers = [at(dx=1), at(dx=-1), at(dy=1), at(dy=-1), at(dc=1)]
    peers += [at(dz=d) for d in (1, -1, 2, -2)]
    for device in peers:
        pl.semaphore_signal(barrier, inc=1, device_id=device, device_id_type=pl.DeviceIdType.MESH)
    pl.semaphore_wait(barrier, len(peers))

    up, down, other = at(dz=1), at(dz=-1), at(dc=1)

    def z_push(i, k, slot, ref, device):
        push(ref, ref, z_s.at[0], ag_r.at[i, k, slot], device)

    def z_share(i, k, zz):
        ref = block(i, k, zz, core)
        push(ref, ref, z_s.at[1], ag_r.at[i, k, 0], other)

    def z_arrived(i, k, slot, ref):
        arrived(ref, z_s.at[0], ag_r.at[i, k, slot])

    def gather_start(i, k):
        row_loads[i][k].wait()
        z_share(i, k, z)
        for d in (2, -2, 1, -1):
            z_push(i, k, d % DEPTH, block(i, k, z, core), at(dz=d))

    def gather_step(i, k, d):
        n = d if d < 4 else d - DEPTH
        ref = block(i, k, z - n, core)
        z_arrived(i, k, d, ref)
        if abs(n) == 1:
            z_push(i, k, 3 * n % DEPTH, ref, at(dz=2 * n))
        elif abs(n) == 2:
            z_push(i, k, 4, ref.at[pl.ds(0 if n > 0 else OWN // 2, OWN // 2)], at(dz=n))
        z_share(i, k, z - n)

    def gather_end(i, k):
        arrived(rows.at[i, k, :, 1 - core], z_s.at[1], ag_r.at[i, k, 0])

    def keep(mask, i, j):
        return mask[i, j].astype(F32)

    def mask_weight(n):
        for load in (other_loads[n], other_loads[3 + n]):
            load.wait()
        ref = weight_d if n == 2 else weights.at[n]
        n_rows, n_cols = (7, 4) if n == 2 else (4, 7)

        def body(i, carry):
            rows_i = pl.ds(pl.multiple_of(i * SIDE, SIDE), SIDE)
            for j in range(n_cols):
                cols = pl.ds(j * SIDE, SIDE)
                factor = keep(dmask, j, i) if n == 2 else keep((gmask, umask)[n], i, j)
                ref[rows_i, cols] = (ref[rows_i, cols].astype(F32) * factor).astype(BF)
            return carry

        lax.fori_loop(0, n_rows, body, 0)

    def tiles(body):
        def step(i, carry):
            body(i, pl.ds(pl.multiple_of(i * 256, 256), 256))
            return carry

        lax.fori_loop(0, MANY // 256, step, 0)

    def tile_rows(j, k, i):
        n = 256 // (2 * OWN)
        return rows[j, k, pl.ds(n * i, n)].reshape(256, 512)

    def partial(a, k):
        def body(i, where):
            if a < 2:
                part[a, k, where] = mm(tile_rows(0, k, i), weights[a], ((1,), (0,)))
            else:
                part[2, k, where] = mm(tile_rows(1, k, i), weight_d[...], ((1,), (1,)))

        tiles(body)

    def ring(h, phase):
        if (h + phase) % 2 == 0:
            return x, at(dx=1), at(dx=-1)
        return y, at(dy=1), at(dy=-1)

    def rs_refs(u, k, h, phase):
        which = SUMS[u]
        if phase == 0:
            return (
                part.at[which, k], h * (MANY // 2), MANY // 16,
                sent1.at[which, k, h], got1.at[which, k, h], acc1.at[which, k, h],
            )
        return (
            acc1.at[which, k, h], 0, MANY // 64,
            sent2.at[which, k, h], got2.at[which, k, h], fin.at[which, k, h],
        )

    def rs_sems(u, k, h, phase, n):
        return rs_s.at[phase], rs_r.at[u, k, h, 3 * phase + n]

    def rs_push(u, k, h, phase, first, count, n, device):
        _, _, _, sent, got, _ = rs_refs(u, k, h, phase)
        where = pl.ds(first, count)
        push(sent.at[:, where], got.at[:, where], *rs_sems(u, k, h, phase, n), device)

    def rs_arrived(u, k, h, phase, first, count, n):
        got = rs_refs(u, k, h, phase)[4]
        arrived(got.at[:, pl.ds(first, count)], *rs_sems(u, k, h, phase, n))

    def rs_block(u, k, h, phase, d, second):
        src, base, n, _, _, _ = rs_refs(u, k, h, phase)
        start = base + 2 * n * d + n * second
        return src[:, pl.ds(pl.multiple_of(start, n), n), :]

    def rs_first(u, k, h, phase):
        q, right, left = ring(h, phase)
        sent = rs_refs(u, k, h, phase)[3]
        dtype = PHASE_DTYPES[phase]
        slots = SLOTS[phase]
        far, to_r, to_l = wrap(q + 2, RING), wrap(q + 1, RING), wrap(q - 1, RING)
        plan = (
            ("FAR_R", far, 0, right, 0), ("FAR_L", far, 1, left, 1),
            ("OWN_R", to_r, 1, right, 2), ("OWN_L", to_l, 0, left, 2),
        )
        for name, d, second, device, n in plan:
            sent[:, slots[name]] = rs_block(u, k, h, phase, d, second).astype(dtype)
            if phase == 0:
                rs_push(u, k, h, 0, slots[name], 1, n, device)
            elif n == 2:
                rs_push(u, k, h, 1, slots[name] - 1, 2, 0 if device is right else 1, device)

    def rs_second(u, k, h, phase):
        q, right, left = ring(h, phase)
        _, _, _, sent, got, _ = rs_refs(u, k, h, phase)
        dtype = PHASE_DTYPES[phase]
        slots = SLOTS[phase]
        for way, d, second, device, n in (
            ("_R", wrap(q + 1, RING), 0, right, 0), ("_L", wrap(q - 1, RING), 1, left, 1),
        ):
            far, out = slots["FAR" + way], slots["SUM" + way]
            rs_arrived(u, k, h, phase, far, 1 + phase, n)
            sent[:, out] = (rs_block(u, k, h, phase, d, second) + got[:, far].astype(F32)).astype(dtype)
            rs_push(u, k, h, phase, out, 1, 2, device)

    def rs_last(u, k, h, phase):
        q = ring(h, phase)[0]
        _, _, n, _, got, dst = rs_refs(u, k, h, phase)
        slots = SLOTS[phase]
        rs_arrived(u, k, h, phase, 2 + 2 * phase, 4 - 2 * phase, 2)
        for second, one, two in ((0, "SUM_R", "OWN_L"), (1, "OWN_R", "SUM_L")):
            dst[:, pl.ds(n * second, n), :] = (
                rs_block(u, k, h, phase, q, second)
                + got[:, slots[one]].astype(F32) + got[:, slots[two]].astype(F32)
            )

    def av_rows(h, phase, d, second=None):
        n = MANY // 32 if phase == 0 else MANY // 8
        start = h * (MANY // 2) + n * d
        if phase == 0:
            start = start + MANY // 8 * ring(h, 0)[0]
        if second is None:
            return pl.ds(pl.multiple_of(start, n), n)
        return pl.ds(pl.multiple_of(start + n // 2 * second, n // 2), n // 2)

    def av_move(v, k, h, phase, slot, where, device=None):
        ref = acts.at[ACTS[v], k, where]
        sems = av_s.at[0], av_r.at[v, k, h, 3 * phase + slot]
        if device is None:
            arrived(ref, *sems)
        else:
            push(ref, ref, *sems, device)

    def av_first(v, k, h, phase):
        q, right, left = ring(h, 1 - phase)
        if phase == 0:
            av_move(v, k, h, 0, 0, av_rows(h, 0, q), right)
            av_move(v, k, h, 0, 1, av_rows(h, 0, q), left)
            return
        for slot, part_of, device in ((0, 0, right), (1, 1, left), (3, 1, right), (4, 0, left)):
            av_move(v, k, h, 1, slot, av_rows(h, 1, q, part_of), device)

    def av_second(v, k, h, phase):
        q, right, left = ring(h, 1 - phase)
        for slot, d, device, part_of in (
            (0, wrap(q - 1, RING), right, 0), (1, wrap(q + 1, RING), left, 1),
        ):
            av_move(v, k, h, phase, slot, av_rows(h, phase, d, part_of if phase == 1 else None))
            if phase == 1:
                av_move(v, k, h, 1, 2, av_rows(h, 1, d, part_of), device)
            elif (v + k + h) % 2 == slot:
                av_move(v, k, h, 0, 2, av_rows(h, 0, d), device)

    def av_last(v, k, h, phase):
        q = ring(h, 1 - phase)[0]
        if phase == 1:
            av_move(v, k, h, 1, 3, av_rows(h, 1, wrap(q - 1, RING), 1))
            av_move(v, k, h, 1, 4, av_rows(h, 1, wrap(q + 1, RING), 0))
        av_move(v, k, h, phase, 2, av_rows(h, phase, wrap(q + 2, RING)))

    def own_rows(h):
        return av_rows(h, 0, ring(h, 1)[0])

    def hidden(k, h):
        gate = fin[0, k, h]
        acts[0, k, own_rows(h)] = (gate * jax.nn.sigmoid(gate) * fin[1, k, h]).astype(BF)
        av_first(0, k, h, 0)

    def act_grads(k, h):
        gate, upv, grad = fin[0, k, h], fin[1, k, h], fin[2, k, h]
        s = jax.nn.sigmoid(gate)
        acts[1, k, own_rows(h)] = (grad * upv * s * (1.0 + gate * (1.0 - s))).astype(BF)
        acts[2, k, own_rows(h)] = (grad * (gate * s)).astype(BF)
        av_first(1, k, h, 0)

    def feature_part(b, a, k, c):
        cols = pl.ds(c * PIECE, PIECE)
        n = 256 // (2 * OWN)

        def body(i, where):
            if a == 0:
                tile = mm(acts[0, k, where], weight_d[:, cols], ((1,), (0,)))
            else:
                tile = mm(acts[a, k, where], weights[a - 1, cols, :], ((1,), (1,)))
            tile = tile.reshape(n, 2, OWN, PIECE)
            if a == 2:
                tile = tile + outs[b, k, c, pl.ds(n * i, n)]
            outs[b, k, c, pl.ds(n * i, n)] = tile

        tiles(body)
        if a != 1:
            push(outs.at[b, k, c, :, 1 - core], peer.at[b, k, c], ex_s.at[0], ex_r.at[b, k, c], other)

    def zr_move(b, k, c, way, n, send):
        where = pl.ds(0, OWN) if n < 4 else pl.ds(OWN // 2 * way, OWN // 2)
        sems = zr_s.at[n // 4], zr_r.at[b, k, c, 3 * way + n - 2 if n > 1 else 6]
        got = zgot.at[b, k, c, way, n - 1, where]
        if send:
            push(zsent.at[b, k, c, way, n - 1, where], got, *sems, (up, down)[way])
        else:
            arrived(got, *sems)

    def zr_step(b, k, c, n):
        if n == 4:
            arrived(peer.at[b, k, c], ex_s.at[0], ex_r.at[b, k, c])
        for way in range(2):
            target = wrap(z + n if way == 0 else z - n, DEPTH)
            if n == 4:
                where = pl.ds(OWN // 2 * way, OWN // 2)
                zsent[b, k, c, way, 3, where] = (
                    outs[b, k, c, target, core, where] + peer[b, k, c, target, where]
                )
            else:
                zr_move(b, k, c, way, n + 1, False)
                if n == 3:
                    fresh, rest = pl.ds(OWN // 2 * way, OWN // 2), pl.ds(OWN // 2 * (1 - way), OWN // 2)
                    zsent[b, k, c, way, 2, rest] = (
                        outs[b, k, c, target, core, rest] + peer[b, k, c, target, rest]
                    )
                    zsent[b, k, c, way, 2, fresh] = (
                        outs[b, k, c, target, core, fresh] + peer[b, k, c, target, fresh]
                        + zgot[b, k, c, way, 3, fresh]
                    )
                else:
                    zsent[b, k, c, way, n - 1] = (
                        outs[b, k, c, target, core] + peer[b, k, c, target] + zgot[b, k, c, way, n]
                    )
            zr_move(b, k, c, way, n, True)

    def zr_last(b, k, c):
        arrived(zgot.at[b, k, c, :, 0], zr_s.at[0], zr_r.at[b, k, c, 6])
        total = outs[b, k, c, z, core] + peer[b, k, c, z] + zgot[b, k, c, 0, 0] + zgot[b, k, c, 1, 0]
        (o_out, gt_out)[b][pl.ds(OWN * k, OWN), pl.ds(c * PIECE, PIECE)] = total.astype(BF)

    def over_tokens(left, right_side):
        total = mm(left(0).T, right_side(0), ((1,), (0,)))
        for k in range(1, CHUNKS):
            total = total + mm(left(k).T, right_side(k), ((1,), (0,)))
        return total

    def masked_store(out, mask, total, row, flip):
        for r in range(total.shape[0] // SIDE):
            for j in range(total.shape[1] // SIDE):
                factor = keep(mask, j, row + r) if flip else keep(mask, row + r, j)
                out[pl.ds((row + r) * SIDE, SIDE), pl.ds(j * SIDE, SIDE)] = (
                    total[r * SIDE : (r + 1) * SIDE, j * SIDE : (j + 1) * SIDE] * factor
                ).astype(BF)

    def grad_weight(a, i):
        cols = pl.ds(256 * i, 256)
        total = over_tokens(lambda k: rows[0, k, :, :, :, cols].reshape(MANY, 256), lambda k: acts[1 + a, k])
        masked_store((gg_out, gu_out)[a], (gmask, umask)[a], total, 2 * i, False)

    def grad_down(i):
        cols = pl.ds(256 * i, min(256, 896 - 256 * i))
        total = over_tokens(lambda k: acts[0, k, :, cols], lambda k: rows[1, k].reshape(MANY, 512))
        masked_store(gd_out, dmask, total, 2 * i, True)

    steps = dict(
        G=gather_start, N=gather_step, E=gather_end, M=mask_weight, P=partial,
        F=rs_first, S=rs_second, L=rs_last, H=hidden, Q=act_grads,
        A=av_first, B=av_second, C=av_last, T=feature_part, Z=zr_step, Y=zr_last,
        W=grad_weight, D=grad_down,
    )
    for code, *indices in SCHEDULE:
        steps[code](*indices)
    sent_all(rows.at[:, :, pl.ds(0, DEPTH - 1), 0], z_s.at[0])
    sent_all(rows.at[:, :, :, 0], z_s.at[1])
    sent_all(sent1, rs_s.at[0])
    sent_all(sent2, rs_s.at[1])
    sent_all(acts.at[:, :, pl.ds(0, MANY // 16 * 15)], av_s.at[0])
    sent_all(peer, ex_s.at[0])
    sent_all(zsent.at[:, :, :, :, pl.ds(0, 3)], zr_s.at[0])
    sent_all(zsent.at[:, :, :, :, 3, pl.ds(0, OWN // 2)], zr_s.at[1])


def store_kernel(*refs):
    sems = refs[-1]
    copies = [pltpu.make_async_copy(refs[i], refs[5 + i], sems.at[i]) for i in range(5)]
    for copy in copies:
        copy.start()
    for copy in copies:
        copy.wait()


def shards(tokens, grad_output, gate_weight, up_weight, down_weight, gate_mask, up_mask, down_mask):
    anywhere = pl.BlockSpec(memory_space=pl.ANY)
    vmem = pl.BlockSpec(memory_space=pltpu.VMEM)
    dma = pltpu.SemaphoreType.DMA
    d1, d2 = PHASE_DTYPES
    n = CHUNKS
    pieces = 512 // PIECE
    shapes = [(64, 512), (64, 512), (512, 896), (512, 896), (896, 512)]
    results = pl.pallas_call(
        kernel,
        out_shape=[pltpu.VMEM(shape, BF) for shape in shapes],
        in_specs=[anywhere] * 8,
        out_specs=[vmem] * 5,
        scratch_shapes=[
            pltpu.VMEM((2, n, DEPTH, 2, OWN, 512), BF),
            pltpu.VMEM((2, 512, 896), BF),
            pltpu.VMEM((896, 512), BF),
            pltpu.VMEM((3, n, MANY, 896), F32),
            pltpu.VMEM((3, n, 2, 6, MANY // 16, 896), d1),
            pltpu.VMEM((3, n, 2, 6, MANY // 16, 896), d1),
            pltpu.VMEM((3, n, 2, MANY // 8, 896), F32),
            pltpu.VMEM((3, n, 2, 6, MANY // 64, 896), d2),
            pltpu.VMEM((3, n, 2, 6, MANY // 64, 896), d2),
            pltpu.VMEM((3, n, 2, MANY // 32, 896), F32),
            pltpu.VMEM((3, n, MANY, 896), BF),
            pltpu.VMEM((2, n, pieces, 8, 2, OWN, PIECE), F32),
            pltpu.VMEM((2, n, pieces, 8, OWN, PIECE), F32),
            pltpu.VMEM((2, n, pieces, 2, 4, OWN, PIECE), F32),
            pltpu.VMEM((2, n, pieces, 2, 4, OWN, PIECE), F32),
            pltpu.SMEM((4, 7), jnp.int32),
            pltpu.SMEM((4, 7), jnp.int32),
            pltpu.SMEM((4, 7), jnp.int32),
            dma((2,)), dma((2, n, 8)),
            dma((2,)), dma((2, n, 2, 6)),
            dma((1,)), dma((2, n, 2, 8)),
            dma((1,)), dma((2, n, pieces)),
            dma((2,)), dma((2, n, pieces, 7)),
            dma((2 * n + 6,)),
        ],
        compiler_params=pltpu.CompilerParams(
            collective_id=0, has_side_effects=True, vmem_limit_bytes=58_000_000
        ),
        name="ffn",
    )(
        tokens, grad_output, gate_weight, up_weight, down_weight, gate_mask, up_mask, down_mask.T
    )
    return tuple(
        pl.pallas_call(
            store_kernel,
            out_shape=[jax.ShapeDtypeStruct(shape, BF) for shape in shapes],
            in_specs=[anywhere] * 5,
            out_specs=[anywhere] * 5,
            scratch_shapes=[dma((5,))],
            name="store",
        )(*[pltpu.with_memory_space_constraint(result, pltpu.VMEM) for result in results])
    )


def solution(mesh):
    return jax.shard_map(
        shards,
        mesh=mesh,
        in_specs=(
            P("tensor", "dp"),
            P("tensor", "dp"),
            P("dp", "tensor"),
            P("dp", "tensor"),
            P("tensor", "dp"),
            P("dp", "tensor"),
            P("dp", "tensor"),
            P("tensor", "dp"),
        ),
        out_specs=(
            P("tensor", "dp"),
            P("tensor", "dp"),
            P("dp", "tensor"),
            P("dp", "tensor"),
            P("tensor", "dp"),
        ),
        check_vma=False,
    )
```

```python
import jax
import jax.numpy as jnp
from jax import lax
from jax.experimental import pallas as pl
from jax.experimental.pallas import tpu as pltpu
from jax.sharding import PartitionSpec as P

BF = jnp.bfloat16
F32 = jnp.float32
SIDE = 128
RING = 4
DEPTH = 8
CHUNKS = 2
OWN = 64 // CHUNKS
MANY = 1024 // CHUNKS
PIECE = 256
PHASE_DTYPES = (BF, F32)

SLOTS = (
    dict(FAR_R=0, FAR_L=1, OWN_R=2, OWN_L=3, SUM_R=4, SUM_L=5),
    dict(FAR_R=0, OWN_R=1, FAR_L=2, OWN_L=3, SUM_R=4, SUM_L=5),
)
SUMS = (pl.ds(0, 2), pl.ds(2, 1))
ACTS = (pl.ds(0, 1), pl.ds(1, 2))

SCHEDULE = (
    ("G", 0, 0),
    ("G", 1, 0),
    ("M", 0),
    ("M", 1),
    ("M", 2),
    ("N", 0, 0, 1),
    ("N", 0, 0, 7),
    ("N", 0, 0, 6),
    ("N", 0, 0, 2),
    ("N", 1, 0, 1),
    ("N", 1, 0, 2),
    ("N", 1, 0, 6),
    ("N", 1, 0, 7),
    ("G", 0, 1),
    ("N", 0, 0, 3),
    ("N", 0, 0, 5),
    ("N", 0, 0, 4),
    ("E", 0, 0),
    ("P", 1, 0),
    ("N", 1, 0, 3),
    ("P", 0, 0),
    ("N", 1, 0, 4),
    ("F", 0, 0, 0, 0),
    ("N", 1, 0, 5),
    ("F", 0, 0, 1, 0),
    ("N", 0, 1, 1),
    ("N", 0, 1, 2),
    ("N", 0, 1, 6),
    ("N", 0, 1, 7),
    ("G", 1, 1),
    ("E", 1, 0),
    ("P", 2, 0),
    ("F", 1, 0, 0, 0),
    ("F", 1, 0, 1, 0),
    ("S", 0, 0, 0, 0),
    ("S", 0, 0, 1, 0),
    ("N", 0, 1, 3),
    ("N", 0, 1, 4),
    ("N", 0, 1, 5),
    ("N", 1, 1, 1),
    ("N", 1, 1, 2),
    ("E", 0, 1),
    ("P", 1, 1),
    ("N", 1, 1, 6),
    ("N", 1, 1, 7),
    ("P", 0, 1),
    ("S", 1, 0, 0, 0),
    ("S", 1, 0, 1, 0),
    ("F", 0, 1, 0, 0),
    ("F", 0, 1, 1, 0),
    ("L", 0, 0, 0, 0),
    ("F", 0, 0, 0, 1),
    ("L", 0, 0, 1, 0),
    ("F", 0, 0, 1, 1),
    ("N", 1, 1, 3),
    ("L", 1, 0, 0, 0),
    ("N", 1, 1, 4),
    ("F", 1, 0, 0, 1),
    ("L", 1, 0, 1, 0),
    ("F", 1, 0, 1, 1),
    ("N", 1, 1, 5),
    ("E", 1, 1),
    ("P", 2, 1),
    ("F", 1, 1, 0, 0),
    ("S", 0, 1, 1, 0),
    ("S", 0, 1, 0, 0),
    ("F", 1, 1, 1, 0),
    ("S", 0, 0, 1, 1),
    ("S", 0, 0, 0, 1),
    ("S", 1, 0, 1, 1),
    ("S", 1, 0, 0, 1),
    ("S", 1, 1, 0, 0),
    ("L", 0, 1, 1, 0),
    ("F", 0, 1, 1, 1),
    ("S", 1, 1, 1, 0),
    ("L", 0, 1, 0, 0),
    ("F", 0, 1, 0, 1),
    ("L", 0, 0, 1, 1),
    ("H", 0, 1),
    ("L", 0, 0, 0, 1),
    ("H", 0, 0),
    ("L", 1, 0, 1, 1),
    ("Q", 0, 1),
    ("L", 1, 0, 0, 1),
    ("Q", 0, 0),
    ("L", 1, 1, 0, 0),
    ("F", 1, 1, 0, 1),
    ("L", 1, 1, 1, 0),
    ("F", 1, 1, 1, 1),
    ("S", 0, 1, 1, 1),
    ("B", 0, 0, 1, 0),
    ("S", 0, 1, 0, 1),
    ("B", 0, 0, 0, 0),
    ("B", 1, 0, 1, 0),
    ("B", 1, 0, 0, 0),
    ("S", 1, 1, 1, 1),
    ("S", 1, 1, 0, 1),
    ("L", 0, 1, 1, 1),
    ("H", 1, 1),
    ("C", 0, 0, 1, 0),
    ("A", 0, 0, 1, 1),
    ("L", 0, 1, 0, 1),
    ("H", 1, 0),
    ("C", 0, 0, 0, 0),
    ("A", 0, 0, 0, 1),
    ("C", 1, 0, 1, 0),
    ("A", 1, 0, 1, 1),
    ("L", 1, 1, 1, 1),
    ("Q", 1, 1),
    ("C", 1, 0, 0, 0),
    ("A", 1, 0, 0, 1),
    ("L", 1, 1, 0, 1),
    ("Q", 1, 0),
    ("B", 0, 1, 1, 0),
    ("B", 0, 0, 1, 1),
    ("B", 0, 0, 0, 1),
    ("B", 0, 1, 0, 0),
    ("B", 1, 1, 1, 0),
    ("B", 1, 0, 1, 1),
    ("B", 1, 0, 0, 1),
    ("B", 1, 1, 0, 0),
    ("C", 0, 1, 1, 0),
    ("A", 0, 1, 1, 1),
    ("C", 0, 0, 1, 1),
    ("C", 0, 1, 0, 0),
    ("A", 0, 1, 0, 1),
    ("C", 0, 0, 0, 1),
    ("T", 0, 0, 0, 0),
    ("T", 0, 0, 0, 1),
    ("C", 1, 1, 1, 0),
    ("A", 1, 1, 1, 1),
    ("C", 1, 0, 1, 1),
    ("Z", 0, 0, 0, 4),
    ("C", 1, 1, 0, 0),
    ("A", 1, 1, 0, 1),
    ("C", 1, 0, 0, 1),
    ("T", 1, 1, 0, 0),
    ("T", 1, 1, 0, 1),
    ("T", 1, 2, 0, 0),
    ("B", 0, 1, 1, 1),
    ("T", 1, 2, 0, 1),
    ("B", 0, 1, 0, 1),
    ("Z", 0, 0, 1, 4),
    ("Z", 1, 0, 0, 4),
    ("Z", 0, 0, 0, 3),
    ("Z", 1, 0, 1, 4),
    ("B", 1, 1, 1, 1),
    ("Z", 0, 0, 1, 3),
    ("B", 1, 1, 0, 1),
    ("Z", 1, 0, 0, 3),
    ("Z", 0, 0, 0, 2),
    ("Z", 1, 0, 1, 3),
    ("C", 0, 1, 1, 1),
    ("C", 0, 1, 0, 1),
    ("T", 0, 0, 1, 0),
    ("T", 0, 0, 1, 1),
    ("Z", 0, 0, 1, 2),
    ("D", 0),
    ("D", 1),
    ("C", 1, 1, 1, 1),
    ("Z", 1, 0, 0, 2),
    ("D", 2),
    ("Z", 0, 0, 0, 1),
    ("C", 1, 1, 0, 1),
    ("T", 1, 1, 1, 0),
    ("T", 1, 1, 1, 1),
    ("T", 1, 2, 1, 0),
    ("Z", 0, 1, 0, 4),
    ("Z", 0, 1, 1, 4),
    ("Z", 1, 0, 1, 2),
    ("T", 1, 2, 1, 1),
    ("D", 3),
    ("Z", 0, 0, 1, 1),
    ("W", 0, 0),
    ("Z", 1, 1, 0, 4),
    ("Z", 1, 1, 1, 4),
    ("W", 0, 1),
    ("Z", 1, 0, 0, 1),
    ("Z", 0, 1, 0, 3),
    ("Z", 0, 1, 1, 3),
    ("W", 1, 0),
    ("Z", 1, 0, 1, 1),
    ("Z", 1, 1, 0, 3),
    ("W", 1, 1),
    ("Y", 0, 0, 0),
    ("Y", 0, 0, 1),
    ("Y", 1, 0, 0),
    ("Z", 1, 1, 1, 3),
    ("Z", 0, 1, 0, 2),
    ("Z", 0, 1, 1, 2),
    ("Y", 1, 0, 1),
    ("Z", 1, 1, 0, 2),
    ("Z", 1, 1, 1, 2),
    ("Z", 0, 1, 0, 1),
    ("Z", 0, 1, 1, 1),
    ("Z", 1, 1, 0, 1),
    ("Z", 1, 1, 1, 1),
    ("Y", 0, 1, 0),
    ("Y", 0, 1, 1),
    ("Y", 1, 1, 0),
    ("Y", 1, 1, 1),
)


def mm(left, right_side, dims):
    return lax.dot_general(left, right_side, (dims, ((), ())), preferred_element_type=F32)


def kernel(
    tok_in, cot_in, wg_in, wu_in, wd_in, gm_in, um_in, dm_in,
    o_out, gt_out, gg_out, gu_out, gd_out,
    rows, weights, weight_d, part, sent1, got1, acc1, sent2, got2, fin,
    acts, outs, peer, zsent, zgot, gmask, umask, dmask,
    z_s, ag_r, rs_s, rs_r, av_s, av_r, ex_s, ex_r, zr_s, zr_r, loc,
):
    dp = lax.axis_index("dp")
    tensor = lax.axis_index("tensor")
    x, y = dp // RING, dp % RING
    z, core = tensor // 2, tensor % 2

    def wrap(value, n):
        return lax.rem(value + 2 * n, n)

    def at(dx=0, dy=0, dz=0, dc=0):
        return {
            "dp": wrap(x + dx, RING) * RING + wrap(y + dy, RING),
            "tensor": wrap(z + dz, DEPTH) * 2 + (1 - core if dc else core),
        }

    def remote(src, dst, s_sem, r_sem, device):
        return pltpu.make_async_remote_copy(
            src_ref=src, dst_ref=dst, send_sem=s_sem, recv_sem=r_sem,
            device_id=device, device_id_type=pl.DeviceIdType.MESH,
        )

    def push(src, dst, s_sem, r_sem, device):
        remote(src, dst, s_sem, r_sem, device).start()

    def arrived(dst, s_sem, r_sem):
        remote(dst, dst, s_sem, r_sem, at(dz=1)).wait_recv()

    def sent_all(src, s_sem):
        remote(src, src, s_sem, ex_r.at[0, 0, 0], at(dz=1)).wait_send()

    def block(i, k, zz, cc):
        return rows.at[i, k, wrap(zz, DEPTH), cc]

    row_loads = [
        [
            pltpu.make_async_copy(
                ref.at[pl.ds(OWN * k, OWN)], block(i, k, z, core), loc.at[CHUNKS * i + k]
            )
            for k in range(CHUNKS)
        ]
        for i, ref in enumerate((tok_in, cot_in))
    ]
    other_loads = [
        pltpu.make_async_copy(src, dst, loc.at[2 * CHUNKS + n])
        for n, (src, dst) in enumerate(
            (
                (gm_in, gmask), (um_in, umask), (dm_in, dmask),
                (wg_in, weights.at[0]), (wu_in, weights.at[1]), (wd_in, weight_d),
            )
        )
    ]
    for load in row_loads[0] + row_loads[1] + other_loads:
        load.start()

    barrier = pltpu.get_barrier_semaphore()
    peers = [at(dx=1), at(dx=-1), at(dy=1), at(dy=-1), at(dc=1)]
    peers += [at(dz=d) for d in (1, -1, 2, -2)]
    for device in peers:
        pl.semaphore_signal(barrier, inc=1, device_id=device, device_id_type=pl.DeviceIdType.MESH)
    pl.semaphore_wait(barrier, len(peers))

    up, down, other = at(dz=1), at(dz=-1), at(dc=1)

    def z_push(i, k, slot, ref, device):
        push(ref, ref, z_s.at[0], ag_r.at[i, k, slot], device)

    def z_share(i, k, zz):
        ref = block(i, k, zz, core)
        push(ref, ref, z_s.at[1], ag_r.at[i, k, 0], other)

    def z_arrived(i, k, slot, ref):
        arrived(ref, z_s.at[0], ag_r.at[i, k, slot])

    def gather_start(i, k):
        row_loads[i][k].wait()
        z_share(i, k, z)
        for d in (2, -2, 1, -1):
            z_push(i, k, d % DEPTH, block(i, k, z, core), at(dz=d))

    def gather_step(i, k, d):
        n = d if d < 4 else d - DEPTH
        ref = block(i, k, z - n, core)
        z_arrived(i, k, d, ref)
        if abs(n) == 1:
            z_push(i, k, 3 * n % DEPTH, ref, at(dz=2 * n))
        elif abs(n) == 2:
            z_push(i, k, 4, ref.at[pl.ds(0 if n > 0 else OWN // 2, OWN // 2)], at(dz=n))
        z_share(i, k, z - n)

    def gather_end(i, k):
        arrived(rows.at[i, k, :, 1 - core], z_s.at[1], ag_r.at[i, k, 0])

    def keep(mask, i, j):
        return mask[i, j].astype(F32)

    def mask_weight(n):
        for load in (other_loads[n], other_loads[3 + n]):
            load.wait()
        ref = weight_d if n == 2 else weights.at[n]
        n_rows, n_cols = (7, 4) if n == 2 else (4, 7)

        def body(i, carry):
            rows_i = pl.ds(pl.multiple_of(i * SIDE, SIDE), SIDE)
            for j in range(n_cols):
                cols = pl.ds(j * SIDE, SIDE)
                factor = keep(dmask, j, i) if n == 2 else keep((gmask, umask)[n], i, j)
                ref[rows_i, cols] = (ref[rows_i, cols].astype(F32) * factor).astype(BF)
            return carry

        lax.fori_loop(0, n_rows, body, 0)

    def tiles(body):
        def step(i, carry):
            body(i, pl.ds(pl.multiple_of(i * 256, 256), 256))
            return carry

        lax.fori_loop(0, MANY // 256, step, 0)

    def tile_rows(j, k, i):
        n = 256 // (2 * OWN)
        return rows[j, k, pl.ds(n * i, n)].reshape(256, 512)

    def partial(a, k):
        def body(i, where):
            if a < 2:
                part[a, k, where] = mm(tile_rows(0, k, i), weights[a], ((1,), (0,)))
            else:
                part[2, k, where] = mm(tile_rows(1, k, i), weight_d[...], ((1,), (1,)))

        tiles(body)

    def ring(h, phase):
        if (h + phase) % 2 == 0:
            return x, at(dx=1), at(dx=-1)
        return y, at(dy=1), at(dy=-1)

    def rs_refs(u, k, h, phase):
        which = SUMS[u]
        if phase == 0:
            return (
                part.at[which, k], h * (MANY // 2), MANY // 16,
                sent1.at[which, k, h], got1.at[which, k, h], acc1.at[which, k, h],
            )
        return (
            acc1.at[which, k, h], 0, MANY // 64,
            sent2.at[which, k, h], got2.at[which, k, h], fin.at[which, k, h],
        )

    def rs_sems(u, k, h, phase, n):
        return rs_s.at[phase], rs_r.at[u, k, h, 3 * phase + n]

    def rs_push(u, k, h, phase, first, count, n, device):
        _, _, _, sent, got, _ = rs_refs(u, k, h, phase)
        where = pl.ds(first, count)
        push(sent.at[:, where], got.at[:, where], *rs_sems(u, k, h, phase, n), device)

    def rs_arrived(u, k, h, phase, first, count, n):
        got = rs_refs(u, k, h, phase)[4]
        arrived(got.at[:, pl.ds(first, count)], *rs_sems(u, k, h, phase, n))

    def rs_block(u, k, h, phase, d, second):
        src, base, n, _, _, _ = rs_refs(u, k, h, phase)
        start = base + 2 * n * d + n * second
        return src[:, pl.ds(pl.multiple_of(start, n), n), :]

    def rs_first(u, k, h, phase):
        q, right, left = ring(h, phase)
        sent = rs_refs(u, k, h, phase)[3]
        dtype = PHASE_DTYPES[phase]
        slots = SLOTS[phase]
        far, to_r, to_l = wrap(q + 2, RING), wrap(q + 1, RING), wrap(q - 1, RING)
        plan = (
            ("FAR_R", far, 0, right, 0), ("FAR_L", far, 1, left, 1),
            ("OWN_R", to_r, 1, right, 2), ("OWN_L", to_l, 0, left, 2),
        )
        for name, d, second, device, n in plan:
            sent[:, slots[name]] = rs_block(u, k, h, phase, d, second).astype(dtype)
            if phase == 0:
                rs_push(u, k, h, 0, slots[name], 1, n, device)
            elif n == 2:
                rs_push(u, k, h, 1, slots[name] - 1, 2, 0 if device is right else 1, device)

    def rs_second(u, k, h, phase):
        q, right, left = ring(h, phase)
        _, _, _, sent, got, _ = rs_refs(u, k, h, phase)
        dtype = PHASE_DTYPES[phase]
        slots = SLOTS[phase]
        for way, d, second, device, n in (
            ("_R", wrap(q + 1, RING), 0, right, 0), ("_L", wrap(q - 1, RING), 1, left, 1),
        ):
            far, out = slots["FAR" + way], slots["SUM" + way]
            rs_arrived(u, k, h, phase, far, 1 + phase, n)
            sent[:, out] = (rs_block(u, k, h, phase, d, second) + got[:, far].astype(F32)).astype(dtype)
            rs_push(u, k, h, phase, out, 1, 2, device)

    def rs_last(u, k, h, phase):
        q = ring(h, phase)[0]
        _, _, n, _, got, dst = rs_refs(u, k, h, phase)
        slots = SLOTS[phase]
        rs_arrived(u, k, h, phase, 2 + 2 * phase, 4 - 2 * phase, 2)
        for second, one, two in ((0, "SUM_R", "OWN_L"), (1, "OWN_R", "SUM_L")):
            dst[:, pl.ds(n * second, n), :] = (
                rs_block(u, k, h, phase, q, second)
                + got[:, slots[one]].astype(F32) + got[:, slots[two]].astype(F32)
            )

    def av_rows(h, phase, d, second=None):
        n = MANY // 32 if phase == 0 else MANY // 8
        start = h * (MANY // 2) + n * d
        if phase == 0:
            start = start + MANY // 8 * ring(h, 0)[0]
        if second is None:
            return pl.ds(pl.multiple_of(start, n), n)
        return pl.ds(pl.multiple_of(start + n // 2 * second, n // 2), n // 2)

    def av_move(v, k, h, phase, slot, where, device=None):
        ref = acts.at[ACTS[v], k, where]
        sems = av_s.at[0], av_r.at[v, k, h, 3 * phase + slot]
        if device is None:
            arrived(ref, *sems)
        else:
            push(ref, ref, *sems, device)

    def av_first(v, k, h, phase):
        q, right, left = ring(h, 1 - phase)
        if phase == 0:
            av_move(v, k, h, 0, 0, av_rows(h, 0, q), right)
            av_move(v, k, h, 0, 1, av_rows(h, 0, q), left)
            return
        for slot, part_of, device in ((0, 0, right), (1, 1, left), (3, 1, right), (4, 0, left)):
            av_move(v, k, h, 1, slot, av_rows(h, 1, q, part_of), device)

    def av_second(v, k, h, phase):
        q, right, left = ring(h, 1 - phase)
        for slot, d, device, part_of in (
            (0, wrap(q - 1, RING), right, 0), (1, wrap(q + 1, RING), left, 1),
        ):
            av_move(v, k, h, phase, slot, av_rows(h, phase, d, part_of if phase == 1 else None))
            if phase == 1:
                av_move(v, k, h, 1, 2, av_rows(h, 1, d, part_of), device)
            elif (v + k + h) % 2 == slot:
                av_move(v, k, h, 0, 2, av_rows(h, 0, d), device)

    def av_last(v, k, h, phase):
        q = ring(h, 1 - phase)[0]
        if phase == 1:
            av_move(v, k, h, 1, 3, av_rows(h, 1, wrap(q - 1, RING), 1))
            av_move(v, k, h, 1, 4, av_rows(h, 1, wrap(q + 1, RING), 0))
        av_move(v, k, h, phase, 2, av_rows(h, phase, wrap(q + 2, RING)))

    def own_rows(h):
        return av_rows(h, 0, ring(h, 1)[0])

    def hidden(k, h):
        gate = fin[0, k, h]
        acts[0, k, own_rows(h)] = (gate * jax.nn.sigmoid(gate) * fin[1, k, h]).astype(BF)
        av_first(0, k, h, 0)

    def act_grads(k, h):
        gate, upv, grad = fin[0, k, h], fin[1, k, h], fin[2, k, h]
        s = jax.nn.sigmoid(gate)
        acts[1, k, own_rows(h)] = (grad * upv * s * (1.0 + gate * (1.0 - s))).astype(BF)
        acts[2, k, own_rows(h)] = (grad * (gate * s)).astype(BF)
        av_first(1, k, h, 0)

    def feature_part(b, a, k, c):
        cols = pl.ds(c * PIECE, PIECE)
        n = 256 // (2 * OWN)

        def body(i, where):
            if a == 0:
                tile = mm(acts[0, k, where], weight_d[:, cols], ((1,), (0,)))
            else:
                tile = mm(acts[a, k, where], weights[a - 1, cols, :], ((1,), (1,)))
            tile = tile.reshape(n, 2, OWN, PIECE)
            if a == 2:
                tile = tile + outs[b, k, c, pl.ds(n * i, n)]
            outs[b, k, c, pl.ds(n * i, n)] = tile

        tiles(body)
        if a != 1:
            push(outs.at[b, k, c, :, 1 - core], peer.at[b, k, c], ex_s.at[0], ex_r.at[b, k, c], other)

    def zr_move(b, k, c, way, n, send):
        where = pl.ds(0, OWN) if n < 4 else pl.ds(OWN // 2 * way, OWN // 2)
        sems = zr_s.at[n // 4], zr_r.at[b, k, c, 3 * way + n - 2 if n > 1 else 6]
        got = zgot.at[b, k, c, way, n - 1, where]
        if send:
            push(zsent.at[b, k, c, way, n - 1, where], got, *sems, (up, down)[way])
        else:
            arrived(got, *sems)

    def zr_step(b, k, c, n):
        if n == 4:
            arrived(peer.at[b, k, c], ex_s.at[0], ex_r.at[b, k, c])
        for way in range(2):
            target = wrap(z + n if way == 0 else z - n, DEPTH)
            if n == 4:
                where = pl.ds(OWN // 2 * way, OWN // 2)
                zsent[b, k, c, way, 3, where] = (
                    outs[b, k, c, target, core, where] + peer[b, k, c, target, where]
                )
            else:
                zr_move(b, k, c, way, n + 1, False)
                if n == 3:
                    fresh, rest = pl.ds(OWN // 2 * way, OWN // 2), pl.ds(OWN // 2 * (1 - way), OWN // 2)
                    zsent[b, k, c, way, 2, rest] = (
                        outs[b, k, c, target, core, rest] + peer[b, k, c, target, rest]
                    )
                    zsent[b, k, c, way, 2, fresh] = (
                        outs[b, k, c, target, core, fresh] + peer[b, k, c, target, fresh]
                        + zgot[b, k, c, way, 3, fresh]
                    )
                else:
                    zsent[b, k, c, way, n - 1] = (
                        outs[b, k, c, target, core] + peer[b, k, c, target] + zgot[b, k, c, way, n]
                    )
            zr_move(b, k, c, way, n, True)

    def zr_last(b, k, c):
        arrived(zgot.at[b, k, c, :, 0], zr_s.at[0], zr_r.at[b, k, c, 6])
        total = outs[b, k, c, z, core] + peer[b, k, c, z] + zgot[b, k, c, 0, 0] + zgot[b, k, c, 1, 0]
        (o_out, gt_out)[b][pl.ds(OWN * k, OWN), pl.ds(c * PIECE, PIECE)] = total.astype(BF)

    def over_tokens(left, right_side):
        total = mm(left(0).T, right_side(0), ((1,), (0,)))
        for k in range(1, CHUNKS):
            total = total + mm(left(k).T, right_side(k), ((1,), (0,)))
        return total

    def masked_store(out, mask, total, row, flip):
        for r in range(total.shape[0] // SIDE):
            for j in range(total.shape[1] // SIDE):
                factor = keep(mask, j, row + r) if flip else keep(mask, row + r, j)
                out[pl.ds((row + r) * SIDE, SIDE), pl.ds(j * SIDE, SIDE)] = (
                    total[r * SIDE : (r + 1) * SIDE, j * SIDE : (j + 1) * SIDE] * factor
                ).astype(BF)

    def grad_weight(a, i):
        cols = pl.ds(256 * i, 256)
        total = over_tokens(lambda k: rows[0, k, :, :, :, cols].reshape(MANY, 256), lambda k: acts[1 + a, k])
        masked_store((gg_out, gu_out)[a], (gmask, umask)[a], total, 2 * i, False)

    def grad_down(i):
        cols = pl.ds(256 * i, min(256, 896 - 256 * i))
        total = over_tokens(lambda k: acts[0, k, :, cols], lambda k: rows[1, k].reshape(MANY, 512))
        masked_store(gd_out, dmask, total, 2 * i, True)

    steps = dict(
        G=gather_start, N=gather_step, E=gather_end, M=mask_weight, P=partial,
        F=rs_first, S=rs_second, L=rs_last, H=hidden, Q=act_grads,
        A=av_first, B=av_second, C=av_last, T=feature_part, Z=zr_step, Y=zr_last,
        W=grad_weight, D=grad_down,
    )
    for code, *indices in SCHEDULE:
        steps[code](*indices)
    sent_all(rows.at[:, :, pl.ds(0, DEPTH - 1), 0], z_s.at[0])
    sent_all(rows.at[:, :, :, 0], z_s.at[1])
    sent_all(sent1, rs_s.at[0])
    sent_all(sent2, rs_s.at[1])
    sent_all(acts.at[:, :, pl.ds(0, MANY // 16 * 15)], av_s.at[0])
    sent_all(peer, ex_s.at[0])
    sent_all(zsent.at[:, :, :, :, pl.ds(0, 3)], zr_s.at[0])
    sent_all(zsent.at[:, :, :, :, 3, pl.ds(0, OWN // 2)], zr_s.at[1])


def store_kernel(*refs):
    sems = refs[-1]
    copies = [pltpu.make_async_copy(refs[i], refs[5 + i], sems.at[i]) for i in range(5)]
    for copy in copies:
        copy.start()
    for copy in copies:
        copy.wait()


def shards(tokens, grad_output, gate_weight, up_weight, down_weight, gate_mask, up_mask, down_mask):
    anywhere = pl.BlockSpec(memory_space=pl.ANY)
    vmem = pl.BlockSpec(memory_space=pltpu.VMEM)
    dma = pltpu.SemaphoreType.DMA
    d1, d2 = PHASE_DTYPES
    n = CHUNKS
    pieces = 512 // PIECE
    shapes = [(64, 512), (64, 512), (512, 896), (512, 896), (896, 512)]
    results = pl.pallas_call(
        kernel,
        out_shape=[pltpu.VMEM(shape, BF) for shape in shapes],
        in_specs=[anywhere] * 8,
        out_specs=[vmem] * 5,
        scratch_shapes=[
            pltpu.VMEM((2, n, DEPTH, 2, OWN, 512), BF),
            pltpu.VMEM((2, 512, 896), BF),
            pltpu.VMEM((896, 512), BF),
            pltpu.VMEM((3, n, MANY, 896), F32),
            pltpu.VMEM((3, n, 2, 6, MANY // 16, 896), d1),
            pltpu.VMEM((3, n, 2, 6, MANY // 16, 896), d1),
            pltpu.VMEM((3, n, 2, MANY // 8, 896), F32),
            pltpu.VMEM((3, n, 2, 6, MANY // 64, 896), d2),
            pltpu.VMEM((3, n, 2, 6, MANY // 64, 896), d2),
            pltpu.VMEM((3, n, 2, MANY // 32, 896), F32),
            pltpu.VMEM((3, n, MANY, 896), BF),
            pltpu.VMEM((2, n, pieces, 8, 2, OWN, PIECE), F32),
            pltpu.VMEM((2, n, pieces, 8, OWN, PIECE), F32),
            pltpu.VMEM((2, n, pieces, 2, 4, OWN, PIECE), F32),
            pltpu.VMEM((2, n, pieces, 2, 4, OWN, PIECE), F32),
            pltpu.SMEM((4, 7), jnp.int32),
            pltpu.SMEM((4, 7), jnp.int32),
            pltpu.SMEM((4, 7), jnp.int32),
            dma((2,)), dma((2, n, 8)),
            dma((2,)), dma((2, n, 2, 6)),
            dma((1,)), dma((2, n, 2, 8)),
            dma((1,)), dma((2, n, pieces)),
            dma((2,)), dma((2, n, pieces, 7)),
            dma((2 * n + 6,)),
        ],
        compiler_params=pltpu.CompilerParams(
            collective_id=0, has_side_effects=True, vmem_limit_bytes=58_000_000
        ),
        name="ffn",
    )(
        tokens, grad_output, gate_weight, up_weight, down_weight, gate_mask, up_mask, down_mask.T
    )
    return tuple(
        pl.pallas_call(
            store_kernel,
            out_shape=[jax.ShapeDtypeStruct(shape, BF) for shape in shapes],
            in_specs=[anywhere] * 5,
            out_specs=[anywhere] * 5,
            scratch_shapes=[dma((5,))],
            name="store",
        )(*[pltpu.with_memory_space_constraint(result, pltpu.VMEM) for result in results])
    )


def solution(mesh):
    return jax.shard_map(
        shards,
        mesh=mesh,
        in_specs=(
            P("tensor", "dp"),
            P("tensor", "dp"),
            P("dp", "tensor"),
            P("dp", "tensor"),
            P("tensor", "dp"),
            P("dp", "tensor"),
            P("dp", "tensor"),
            P("tensor", "dp"),
        ),
        out_specs=(
            P("tensor", "dp"),
            P("tensor", "dp"),
            P("dp", "tensor"),
            P("dp", "tensor"),
            P("tensor", "dp"),
        ),
        check_vma=False,
    )
```
